256 devices in a mesh: row: 2 (over core), sector: 32 (over z, y), slab: 4 (over x).
Axes of the slice: x: 4, y: 4, z: 8, core: 2. Of those that a mesh axis runs over, the one named last changes fastest.
Arguments:
- state: float32 [2, 5, 32, 1024, 128], P('row', None, 'slab', 'sector'), may hold values from -6 to 6
- source: float32 [2, 5, 32, 1024, 128], P('row', None, 'slab', 'sector'), may hold values from -6 to 6
- diag_inverse: float32 [2, 5, 5, 32, 1024, 128], P('row', None, None, 'slab', 'sector'), may hold values from -1 to 1
- jac_axial: float32 [2, 5, 5], P('row'), may hold values from -1 to 2
- jac_cross: float32 [2, 2, 5, 5], P('row'), may hold values from -2.5 to 2.5
- owner: int32 [1024], replicated, may hold values from 0 to 1023, as said below
Outputs:
- residual: float32 [2, 5, 32, 1024, 128], P('row', None, 'slab', 'sector')
- new_state: float32 [2, 5, 32, 1024, 128], P('row', None, 'slab', 'sector')
The draws below stay inside these ranges and needn't reach their ends.
Inputs may be any that keep to these rules, and one draw needn't show every extreme that they name: owner is a permutation; for some whole s, the columns b * 32 to b * 32 + 31 of the rotor face exactly the stator columns s + b * 32 to s + b * 32 + 31, taken modulo 1024, for every b.
All inputs are finite; a program needn't handle non-finite values.
Results may differ from the reference program's by a relative error of at most 0.0001.
Values sent between devices are 32-bit elements; how exact they have to be, the bound alone decides.
No kernel may reach another device: no remote copies, remote signals or barrier semaphores. Data moves between devices by JAX's collectives and lax.ppermute only.
A program may use at most 64 MiB of HBM per device.

```python
import jax
import jax.numpy as jnp
from jax import lax

VARS = 5
C = 32
R = 128
AXIAL_PLANES = 32
NC = 1024


def draw_diag_inverse(key, part):
    first, second, third, fourth = jax.random.split(jax.random.fold_in(key, 11), 4)
    doubling_level = jax.random.uniform(first, (2, AXIAL_PLANES, NC, R), jnp.float32, 0.92, 1.0)
    plane_positions = jax.random.randint(second, (2, 3), 0, AXIAL_PLANES)
    sweep_group = jnp.any(jnp.arange(AXIAL_PLANES)[None, :, None] == plane_positions[:, None, :], axis=2)
    doubling_level = doubling_level * jnp.where(sweep_group, 0.6, 1.0)[:, :, None, None]
    vary = jax.random.uniform(fourth, (2, 5, AXIAL_PLANES, NC, R), jnp.float32, 0.85, 1.0)
    diagonal = doubling_level[:, None] * vary
    noise = 0.06 * jax.random.normal(third, (2, 5, 5, AXIAL_PLANES, NC, R), jnp.float32)
    identity = jnp.eye(5, dtype=jnp.float32)[None, :, :, None, None, None]
    return identity * diagonal[:, :, None] + (1.0 - identity) * noise


def draw_jac_axial(key, part):
    first, second = jax.random.split(jax.random.fold_in(key, 17), 2)
    rates = jax.random.uniform(first, (2, 5), jnp.float32, 0.9, 0.98)
    noise = 0.08 * jax.random.normal(second, (2, 5, 5), jnp.float32)
    identity = jnp.eye(5, dtype=jnp.float32)[None]
    return identity * (2.0 * rates)[:, :, None] + (1.0 - identity) * noise


def draw_owner(key, part):
    first, second = jax.random.split(jax.random.fold_in(key, 23), 2)
    offset = jax.random.randint(first, (), 0, NC)
    blocks = NC // C
    scores = jax.random.randint(second, (blocks, C), 0, 2 ** 20) * C + jnp.arange(C, dtype=jnp.int32)[None, :]
    within = jnp.argsort(scores, axis=1).astype(jnp.int32)
    starts = jnp.arange(blocks, dtype=jnp.int32)[:, None] * C
    return ((offset + starts + within) % NC).reshape(NC).astype(jnp.int32)


def steps_of(own_key, dims, cuts, smallest, high):
    def one(dim, blocks):
        draws = jax.random.uniform(jax.random.fold_in(jax.random.fold_in(own_key, 6), dim), (blocks,), jnp.float32, smallest / len(cuts), high / len(cuts))
        return jnp.repeat(jnp.exp(draws), dims[dim] // blocks).reshape((-1,) + (1,) * (len(dims) - dim - 1))

    loudness = one(*cuts[0])
    for cut in cuts[1:]:
        loudness = loudness * one(*cut)
    return loudness


def normal_values(stream_key, dims, scale, limit, pieces=(), kind=jnp.bfloat16):
    factor_of = steps_of(stream_key, dims, pieces, -0.22, 0.18) if pieces else 1.0
    entries = jax.random.normal(stream_key, dims, jnp.float32) * scale * factor_of
    return jnp.minimum(jnp.maximum(entries, -limit), limit).astype(kind)


def setup_inputs(seed: int = 0) -> dict:
    seeds = jax.random.split(jax.random.key(seed), 7)
    return {
        "state": normal_values(seeds[0], (2, VARS, AXIAL_PLANES, NC, R), 1.0, 6.0, ((0, 2), (2, 4), (3, 32)), jnp.float32),
        "source": normal_values(seeds[1], (2, VARS, AXIAL_PLANES, NC, R), 1.0, 6.0, ((0, 2), (2, 4), (3, 32)), jnp.float32),
        "diag_inverse": draw_diag_inverse(jax.random.fold_in(seeds[6], 71), 0),
        "jac_axial": draw_jac_axial(jax.random.fold_in(seeds[6], 71), 0),
        "jac_cross": normal_values(seeds[4], (2, 2, VARS, VARS), VARS ** -0.5, 2.5, ((0, 2),), jnp.float32),
        "owner": draw_owner(jax.random.fold_in(seeds[6], 71), 0),
    }


exact_mode = lax.Precision.HIGHEST


def mix_const(matrix, field):
    return jnp.einsum('ij,j...->i...', matrix, field, precision=exact_mode)


def per_cell(blocks, field):
    return jnp.sum(blocks * field[None], axis=1)


def forward_sweep(residual, inverse, axial, entering):
    planes = residual.shape[1]

    def advance(plane_at, carried):
        previous, output = carried
        block = lax.dynamic_index_in_dim(inverse, plane_at, 2, keepdims=False)
        value = lax.dynamic_index_in_dim(residual, plane_at, 1, keepdims=False)
        present_plane = per_cell(block, value + 0.5 * mix_const(axial, previous))
        output = lax.dynamic_update_index_in_dim(output, present_plane, plane_at, 1)
        return present_plane, output

    final_plane, output = lax.fori_loop(0, planes, advance, (entering, jnp.zeros_like(residual)))
    return output


def backward_sweep(provisional, inverse, axial, entering):
    planes = provisional.shape[1]

    def advance(step_at, carried):
        following, output = carried
        plane_at = planes - 1 - step_at
        block = lax.dynamic_index_in_dim(inverse, plane_at, 2, keepdims=False)
        value = lax.dynamic_index_in_dim(provisional, plane_at, 1, keepdims=False)
        present_plane = value - per_cell(block, 0.5 * mix_const(axial, following))
        output = lax.dynamic_update_index_in_dim(output, present_plane, plane_at, 1)
        return present_plane, output

    final_plane, output = lax.fori_loop(0, planes, advance, (entering, jnp.zeros_like(provisional)))
    return output


def flux_residual(field, source, axial, circular, radial_jac, below, above):
    axial_padded = jnp.concatenate([below[:, None], field, above[:, None]], axis=1)
    axial_diff = axial_padded[:, 2:] - axial_padded[:, :-2]
    cycle_diff = jnp.roll(field, -1, axis=2) - jnp.roll(field, 1, axis=2)
    radial = jnp.pad(field, ((0, 0), (0, 0), (0, 0), (1, 1)))
    radial_diff = radial[..., 2:] - radial[..., :-2]
    return source - 0.5 * (mix_const(axial, axial_diff) + mix_const(circular, cycle_diff) + mix_const(radial_jac, radial_diff))


def reference(state, source, diag_inverse, jac_axial, jac_cross, owner):
    zeros_plane = jnp.zeros_like(state[0][:, 0])
    rotor_above = jnp.take(state[1][:, 0], owner, axis=1)
    stator_below = zeros_plane.at[:, owner].set(state[0][:, -1])
    bounds = ((zeros_plane, rotor_above), (stator_below, zeros_plane))
    residuals = []
    updated = []
    for blade_row in range(2):
        field = state[blade_row]
        residual = flux_residual(field, source[blade_row], jac_axial[blade_row], jac_cross[blade_row, 0], jac_cross[blade_row, 1], bounds[blade_row][0], bounds[blade_row][1])
        provisional = forward_sweep(residual, diag_inverse[blade_row], jac_axial[blade_row], zeros_plane)
        update = backward_sweep(provisional, diag_inverse[blade_row], jac_axial[blade_row], zeros_plane)
        residuals.append(residual)
        updated.append(field + update)
    return jnp.stack(residuals), jnp.stack(updated)
```

```python
import jax
import jax.numpy as jnp
from jax import lax
from jax.experimental import pallas as pl
from jax.experimental.pallas import tpu as pltpu
from jax.sharding import PartitionSpec as P

F32 = jnp.float32
V = 5
AXES = ("row", "sector", "slab")
VMEM_BYTES = 14 * 1024 * 1024


def matvec(mat, vec):
    out = []
    for i in range(V):
        acc = mat(i, 0) * vec[0]
        for j in range(1, V):
            acc = acc + mat(i, j) * vec[j]
        out.append(acc)
    return out


def stacked(ref, base):
    return lambda i, j: ref[base + V * i + j]


def planes_of(ref, base):
    return [ref[base + v] for v in range(V)]


def put(ref, base, values):
    for v in range(V):
        ref[base + v] = values[v]


def pack_kernel(planes, columns, state, towards_low, interface, towards_high, lowest):
    row = lax.axis_index("row")
    face = jnp.where(row == 0, planes - 1, 0)
    for v in range(V):
        plane = state[0, v, face]
        interface[v] = plane
        towards_low[v, planes:] = plane
        lowest[v] = state[0, v, 0]
        for x in range(planes):
            towards_low[v, x : x + 1] = state[0, v, x, 0:1]
            towards_high[v, x : x + 1] = state[0, v, x, columns - 1 : columns]


def window_kernel(planes, columns, sectors, owner, own, next_one, next_two, message, table, landing):
    row = lax.axis_index("row")
    sector = lax.axis_index("sector")
    total = sectors * columns
    for v in range(V):
        table[v, 0:columns] = own[v]
        table[v, columns : 2 * columns] = next_one[v, planes:]
        table[v, 2 * columns :] = next_two[v]
    lead = owner[0]

    def lower(i, best):
        gap = lax.rem(owner[i] - lead + total + total // 2, total) - total // 2
        return jnp.minimum(best, gap)

    start = lax.rem(lead + lax.fori_loop(0, columns, lower, 0) + total, total)
    turn = start // columns
    even = turn // 2 * 2

    @pl.when(row == 1)
    def _():
        facing = lax.rem(sector - even + sectors, sectors)

        def step(i, carry):
            at = lax.rem(owner[facing * columns + i] - sector * columns + total, total)
            at = jnp.minimum(at, 3 * columns - 1)
            for v in range(V):
                landing[v, pl.ds(i, 1)] = table[v, pl.ds(at, 1)]
            return carry

        lax.fori_loop(0, columns, step, 0, unroll=4)

    @pl.when(row == 0)
    def _():
        facing = lax.rem(sector + even + 2, sectors)
        first = (1 - (turn - even)) * columns

        def step(i, carry):
            at = first + i
            column = owner[lax.rem(sector * columns + at, total)]
            to = lax.rem(column - facing * columns + total, total)
            to = jnp.minimum(to, columns)
            for v in range(V):
                landing[v, pl.ds(to, 1)] = table[v, pl.ds(at, 1)]
            return carry

        lax.fori_loop(0, 2 * columns, step, 0, unroll=4)

    for v in range(V):
        message[v] = landing[v, 0:columns]


def matrix_kernel(planes, axial, inverse, up, down, product, prefix, left, right):
    scaled = [[0.5 * axial[0, i, j] for j in range(V)] for i in range(V)]

    def forward(x, carry):
        for i in range(V):
            entries = [inverse[0, i, k, x] for k in range(V)]
            for j in range(V):
                acc = entries[0] * scaled[0][j]
                for k in range(1, V):
                    acc = acc + entries[k] * scaled[k][j]
                product[x, V * i + j] = acc
        before = jnp.maximum(x - 1, 0)
        for j in range(V):
            column = [
                jnp.where(x == 0, jnp.full((8, 128), float(i == j), F32), prefix[before, V * i + j])
                for i in range(V)
            ]
            put_column(prefix.at[x], j, matvec(stacked(product.at[x], 0), column))
        return carry

    for k in range(V * V):
        prefix[0, k] = jnp.zeros((8, 128), F32)
        left[k] = jnp.zeros((8, 128), F32)
        right[k] = jnp.full((8, 128), float(k // V == k % V), F32)
    lax.fori_loop(0, planes, forward, 0)

    def backward(step, carry):
        x = planes - 1 - step
        before = jnp.maximum(x - 1, 0)
        for j in range(V):
            column = [
                jnp.where(x == 0, jnp.full((8, 128), float(i == j), F32), prefix[before, V * i + j])
                - left[V * i + j]
                for i in range(V)
            ]
            put_column(left, j, matvec(stacked(product.at[x], 0), column))
            column = [-right[V * i + j] for i in range(V)]
            put_column(right, j, matvec(stacked(product.at[x], 0), column))
        return carry

    lax.fori_loop(0, planes, backward, 0)
    for k in range(V * V):
        up[2 * V + k] = prefix[planes - 1, k]
        down[V + k] = right[k]
        down[V + V * V + k] = left[k]


def put_column(ref, j, values):
    for i in range(V):
        ref[V * i + j] = values[i]


def residual_kernel(
    planes, columns, axial, cross, state, source, inverse, from_high, from_low, above, up_in, down_in,
    residual, up, down, wide, forward,
):
    step = pl.program_id(0)

    @pl.when(step == 0)
    def _():
        for v in range(V):
            for x in range(planes):
                wide[v, x, 8 : 8 + columns] = state[0, v, x]
                wide[v, x, 7:8] = from_low[v, x : x + 1]
                wide[v, x, 8 + columns : 9 + columns] = from_high[v, x : x + 1]

    middle = pl.multiple_of(step * 8 + 8, 8)
    low = pl.multiple_of(step * 8, 8)
    high = pl.multiple_of(step * 8 + 16, 8)
    rows = lax.broadcasted_iota(jnp.int32, (8, 128), 0)
    lanes = lax.broadcasted_iota(jnp.int32, (8, 128), 1)
    ja = lambda i, j: 0.5 * axial[0, i, j]
    jb = lambda i, j: 0.5 * cross[0, 0, i, j]
    jr = lambda i, j: 0.5 * cross[0, 1, i, j]
    previous = None
    for x in range(planes):
        along, around, outward = [], [], []
        for v in range(V):
            here = wide[v, x, pl.ds(middle, 8)]
            nearer = wide[v, x + 1, pl.ds(middle, 8)] if x + 1 < planes else above[v]
            along.append(nearer - wide[v, x - 1, pl.ds(middle, 8)] if x else nearer)
            plus = jnp.where(rows == 0, wide[v, x, pl.ds(high, 8)], here)
            minus = jnp.where(rows == 7, wide[v, x, pl.ds(low, 8)], here)
            around.append(pltpu.roll(plus, 7, 0) - pltpu.roll(minus, 1, 0))
            outward.append(
                jnp.where(lanes == 127, 0.0, pltpu.roll(here, 127, 1))
                - jnp.where(lanes == 0, 0.0, pltpu.roll(here, 1, 1))
            )
        one, two, three = matvec(ja, along), matvec(jb, around), matvec(jr, outward)
        values = [source[0, v, x] - (one[v] + two[v] + three[v]) for v in range(V)]
        for v in range(V):
            residual[v, x] = values[v]
        if previous is not None:
            carried = matvec(ja, previous)
            values = [values[v] + carried[v] for v in range(V)]
        previous = matvec(lambda i, j, x=x: inverse[0, i, j, x], values)
        for v in range(V):
            forward[v, x] = previous[v]
    for v in range(V):
        last = wide[v, planes - 1, pl.ds(middle, 8)]
        up[v] = previous[v] + last
        up[V + v] = last
    for x in range(planes - 2, -1, -1):
        carried = matvec(lambda i, j, x=x: inverse[0, i, j, x], matvec(ja, previous))
        previous = [forward[v, x] - carried[v] for v in range(V)]
    for v in range(V):
        down[v] = previous[v]


def first_kernel(slabs, ghost, up, down, entry, message):
    slab = lax.axis_index("slab")
    values = planes_of(ghost, 0)
    for v in range(V):
        message[V + v] = up[V + v]

    @pl.when(slab == 0)
    def _():
        moved = matvec(stacked(up, 2 * V), values)
        for v in range(V):
            total = up[v] + moved[v]
            entry[v] = total
            message[v] = total

    @pl.when(slab != 0)
    def _():
        moved = matvec(stacked(down, V), values)
        for v in range(V):
            entry[v] = up[v]
            message[v] = moved[v]


def middle_kernel(came, came_side, up_other, down_other, up, down, lower, message, entry, leaving):
    slab = lax.axis_index("slab")

    @pl.when(slab == 2)
    def _():
        moved = matvec(stacked(up_other, 2 * V), planes_of(came, 0))
        second = [up_other[v] + moved[v] for v in range(V)]
        moved = matvec(stacked(up, 2 * V), second)
        third = [up[v] + moved[v] for v in range(V)]
        moved = matvec(stacked(down_other, V + V * V), third)
        top = [down_other[v] + came_side[v] + moved[v] for v in range(V)]
        moved = matvec(stacked(down, V + V * V), second)
        again = matvec(stacked(down, V), top)
        put(lower, 0, [down[v] + moved[v] + again[v] for v in range(V)])
        put(message, 0, third)
        put(message, V, planes_of(up, V))
        put(entry, 0, second)
        put(leaving, 0, top)


def last_kernel(
    planes, axial, ghost, came_side, to_third, to_zero, to_one, entry, leaving, zeroth,
    up_other, down_other, partial, inverse, state, residual, new_state, forward, inflow, beyond, under,
):
    row = lax.axis_index("row")
    slab = lax.axis_index("slab")
    ja = lambda i, j: 0.5 * axial[0, i, j]

    @pl.when(slab == 0)
    def _():
        put(inflow, 0, planes_of(ghost, 0))
        put(under, 0, planes_of(ghost, 0))
        one = matvec(stacked(down_other, V + V * V), planes_of(zeroth, 0))
        two = matvec(stacked(down_other, V), planes_of(to_zero, 0))
        put(beyond, 0, [down_other[v] + one[v] + two[v] for v in range(V)])

    @pl.when(slab == 1)
    def _():
        put(inflow, 0, planes_of(came_side, 0))
        put(under, 0, planes_of(came_side, V))
        put(beyond, 0, planes_of(to_one, 0))

    @pl.when(slab == 2)
    def _():
        put(inflow, 0, planes_of(entry, 0))
        put(under, 0, planes_of(up_other, V))
        put(beyond, 0, planes_of(leaving, 0))

    @pl.when(slab == 3)
    def _():
        put(inflow, 0, planes_of(to_third, 0))
        put(under, 0, planes_of(to_third, V))
        put(beyond, 0, [jnp.zeros((8, 128), F32)] * V)

    has_top = jnp.where((row == 0) & (slab == 3), 1.0, 0.0)
    previous = planes_of(inflow, 0)
    for x in range(planes):
        values = [partial[v, x] for v in range(V)]
        if x == planes - 1:
            top = matvec(ja, [ghost[v] * has_top for v in range(V)])
            values = [values[v] - top[v] for v in range(V)]
        if x == 0:
            bottom = matvec(ja, planes_of(under, 0))
            for v in range(V):
                residual[0, v, x] = values[v] + bottom[v]
        else:
            for v in range(V):
                residual[0, v, x] = values[v]
        carried = matvec(ja, previous)
        values = [values[v] + carried[v] for v in range(V)]
        previous = matvec(lambda i, j, x=x: inverse[0, i, j, x], values)
        for v in range(V):
            forward[v, x] = previous[v]
    following = planes_of(beyond, 0)
    for x in range(planes - 1, -1, -1):
        carried = matvec(lambda i, j, x=x: inverse[0, i, j, x], matvec(ja, following))
        following = [forward[v, x] - carried[v] for v in range(V)]
        for v in range(V):
            new_state[0, v, x] = state[0, v, x] + following[v]


def sds(*shape):
    return jax.ShapeDtypeStruct(shape, F32)


def full(shape):
    return pl.BlockSpec(shape, lambda *_: (0,) * len(shape))


def strip(lead):
    return pl.BlockSpec((lead, 8, 128), lambda i: (0, i, 0))


SCALARS = pl.BlockSpec(memory_space=pltpu.SMEM)


def params(**more):
    return pltpu.CompilerParams(vmem_limit_bytes=VMEM_BYTES, **more)


def cost(amount):
    return pl.CostEstimate(flops=amount, bytes_accessed=amount // 8, transcendentals=0)


def per_device(state, source, diag_inverse, jac_axial, jac_cross, owner):
    planes, columns, radial = state.shape[2:]
    sectors = lax.axis_size("sector")
    slabs = lax.axis_size("slab")
    strips = columns // 8
    plane = (V, columns, radial)
    cells = pl.BlockSpec((1, V, planes, 8, radial), lambda i: (0, 0, 0, i, 0))
    blocks = pl.BlockSpec((1, V, V, planes, 8, radial), lambda i: (0, 0, 0, 0, i, 0))
    inner = pl.BlockSpec((V, planes, 8, radial), lambda i: (0, 0, i, 0))
    size = slabs * sectors

    def device(row, sector, slab):
        return row * size + sector % sectors * slabs + slab

    def import_pairs(even):
        pairs = []
        for j in range(sectors):
            pairs.append((device(1, j, 0), device(0, j - even, slabs - 1)))
            pairs.append((device(0, j, slabs - 1), device(1, j + even + 2, 0)))
        return pairs

    two_down = []
    for j in range(sectors):
        two_down.append((device(0, j, slabs - 1), device(0, j - 2, slabs - 1)))
        two_down.append((device(1, j, 0), device(1, j - 2, 0)))

    towards_low, interface, towards_high, lowest = pl.pallas_call(
        lambda *refs: pack_kernel(planes, columns, *refs),
        out_shape=(sds(V, planes + columns, radial), sds(*plane), sds(V, planes, radial), sds(*plane)),
        compiler_params=params(),
        name="pack",
    )(state)
    from_high = lax.ppermute(towards_low, "sector", [(j, (j - 1) % sectors) for j in range(sectors)])
    from_second = lax.ppermute(interface, AXES, two_down)
    from_low = lax.ppermute(towards_high, "sector", [(j, (j + 1) % sectors) for j in range(sectors)])
    above = lax.ppermute(lowest, "slab", [(k, k - 1) for k in range(1, slabs)])

    up, down = pl.pallas_call(
        lambda *refs: matrix_kernel(planes, *refs),
        grid=(strips,),
        in_specs=[SCALARS, blocks],
        out_specs=(strip(2 * V + V * V), strip(V + 2 * V * V)),
        out_shape=(sds(2 * V + V * V, columns, radial), sds(V + 2 * V * V, columns, radial)),
        scratch_shapes=[
            pltpu.VMEM((planes, V * V, 8, radial), F32),
            pltpu.VMEM((planes, V * V, 8, radial), F32),
            pltpu.VMEM((V * V, 8, radial), F32),
            pltpu.VMEM((V * V, 8, radial), F32),
        ],
        compiler_params=params(),
        cost_estimate=cost(80_000_000),
        name="matrices",
    )(jac_axial, diag_inverse)

    message = pl.pallas_call(
        lambda *refs: window_kernel(planes, columns, sectors, *refs),
        in_specs=[SCALARS] + [pl.BlockSpec(memory_space=pltpu.VMEM)] * 3,
        out_shape=sds(*plane),
        scratch_shapes=[
            pltpu.VMEM((V, 3 * columns, radial), F32),
            pltpu.VMEM((V, columns + 8, radial), F32),
        ],
        compiler_params=params(),
        name="window",
    )(owner, interface, from_high, from_second)

    def exchange(even, message, from_low, above, from_high, up, down):
        ghost = lax.ppermute(message, AXES, import_pairs(even))
        partial, up, down = pl.pallas_call(
            lambda *refs: residual_kernel(planes, columns, *refs),
            grid=(strips,),
            in_specs=[
                SCALARS, SCALARS, full(state.shape), cells, blocks,
                full(towards_low.shape), full(towards_high.shape), strip(V),
                pl.BlockSpec(memory_space=pl.ANY), pl.BlockSpec(memory_space=pl.ANY),
            ],
            out_specs=(inner, strip(2 * V), strip(V)),
            out_shape=(sds(V, planes, columns, radial), up, down),
            input_output_aliases={8: 1, 9: 2},
            scratch_shapes=[
                pltpu.VMEM((V, planes, columns + 16, radial), F32),
                pltpu.VMEM((V, planes, 8, radial), F32),
            ],
            compiler_params=params(),
            cost_estimate=cost(40_000_000),
            name="residual",
        )(jac_axial, jac_cross, state, source, diag_inverse, from_high, from_low, above, up, down)
        up_other = lax.ppermute(up, "slab", [(1, 2)])
        down_other = lax.ppermute(down, "slab", [(1, 0), (3, 2)])
        return ghost, partial, up, down, up_other, down_other

    total = sectors * columns
    assert total & (total - 1) == 0
    lead = owner[:columns]
    gaps = ((lead - owner[0] + total // 2) & (total - 1)) - total // 2
    pair = lax.shift_right_logical(
        (owner[0] + jnp.min(gaps)) & (total - 1), jnp.int32((2 * columns).bit_length() - 1)
    )
    ghost, partial, up, down, up_other, down_other = lax.switch(
        pair,
        [lambda *args, e=e: exchange(2 * e, *args) for e in range(sectors // 2)],
        message, from_low, above, from_high, up, down,
    )

    entry, side = pl.pallas_call(
        lambda *refs: first_kernel(slabs, *refs),
        out_shape=(sds(*plane), sds(2 * V, columns, radial)),
        compiler_params=params(),
        name="first",
    )(ghost, up, down)
    came = lax.ppermute(entry, "slab", [(0, 2)])
    came_side = lax.ppermute(side, "slab", [(0, 1), (3, 2)])
    lower, onward, second, top = pl.pallas_call(
        middle_kernel,
        out_shape=(sds(*plane), sds(2 * V, columns, radial), sds(*plane), sds(*plane)),
        compiler_params=params(),
        name="middle",
    )(came, came_side, up_other, down_other, up, down)
    to_zero = lax.ppermute(lower, "slab", [(2, 0)])
    to_one = lax.ppermute(lower, "slab", [(2, 1)])
    to_third = lax.ppermute(onward, "slab", [(2, 3)])

    residual, new_state = pl.pallas_call(
        lambda *refs: last_kernel(planes, *refs),
        grid=(strips,),
        in_specs=[
            SCALARS, strip(V), strip(2 * V), strip(2 * V), strip(V), strip(V), strip(V), strip(V),
            strip(V), strip(2 * V + V * V), strip(V + 2 * V * V), inner, blocks, cells,
        ],
        out_specs=(cells, cells),
        out_shape=(sds(*state.shape), sds(*state.shape)),
        scratch_shapes=[pltpu.VMEM((V, planes, 8, radial), F32)]
        + [pltpu.VMEM((V, 8, radial), F32)] * 3,
        compiler_params=params(),
        name="last",
    )(
        jac_axial, ghost, came_side, to_third, to_zero, to_one, second, top, entry,
        up_other, down_other, partial, diag_inverse, state,
    )
    return residual, new_state


def solution(mesh):
    return jax.shard_map(
        per_device,
        mesh=mesh,
        in_specs=(
            P("row", None, "slab", "sector", None),
            P("row", None, "slab", "sector", None),
            P("row", None, None, "slab", "sector", None),
            P("row", None, None),
            P("row", None, None, None),
            P(),
        ),
        out_specs=(P("row", None, "slab", "sector", None), P("row", None, "slab", "sector", None)),
        check_vma=False,
    )
```

```python
import jax
import jax.numpy as jnp
from jax import lax
from jax.experimental import pallas as pl
from jax.experimental.pallas import tpu as pltpu
from jax.sharding import PartitionSpec as P

F32 = jnp.float32
V = 5
AXES = ("row", "sector", "slab")
VMEM_BYTES = 14 * 1024 * 1024


def matvec(mat, vec):
    out = []
    for i in range(V):
        acc = mat(i, 0) * vec[0]
        for j in range(1, V):
            acc = acc + mat(i, j) * vec[j]
        out.append(acc)
    return out


def stacked(ref, base):
    return lambda i, j: ref[base + V * i + j]


def planes_of(ref, base):
    return [ref[base + v] for v in range(V)]


def put(ref, base, values):
    for v in range(V):
        ref[base + v] = values[v]


def sliding(owner, columns, total):
    lead = owner[0]

    def lower(i, best):
        return jnp.minimum(best, ((owner[i] - lead + total // 2) & (total - 1)) - total // 2)

    return (lead + lax.fori_loop(1, columns, lower, jnp.int32(0), unroll=True)) & (total - 1)


def pack_kernel(planes, columns, owner, state, towards_low, interface, towards_high, lowest, pair):
    row = lax.axis_index("row")
    face = jnp.where(row == 0, planes - 1, 0)
    pair[0] = sliding(owner, columns, owner.shape[0]) >> ((2 * columns).bit_length() - 1)
    for v in range(V):
        plane = state[0, v, face]
        interface[v] = plane
        towards_low[v, planes:] = plane
        lowest[v] = state[0, v, 0]
        for x in range(planes):
            towards_low[v, x : x + 1] = state[0, v, x, 0:1]
            towards_high[v, x : x + 1] = state[0, v, x, columns - 1 : columns]


def window_kernel(planes, columns, sectors, owner, own, next_one, next_two, message, table, landing):
    row = lax.axis_index("row")
    sector = lax.axis_index("sector")
    total = sectors * columns
    for v in range(V):
        table[v, 0:columns] = own[v]
        table[v, columns : 2 * columns] = next_one[v, planes:]
        table[v, 2 * columns :] = next_two[v]
    turn = sliding(owner, columns, total) >> (columns.bit_length() - 1)
    even = turn & -2

    @pl.when(row == 1)
    def _():
        facing = (sector - even) & (sectors - 1)

        def step(i, carry):
            at = (owner[facing * columns + i] - sector * columns) & (total - 1)
            at = jnp.minimum(at, 3 * columns - 1)
            for v in range(V):
                landing[v, pl.ds(i, 1)] = table[v, pl.ds(at, 1)]
            return carry

        lax.fori_loop(0, columns, step, 0, unroll=8)

    @pl.when(row == 0)
    def _():
        facing = (sector + even + 2) & (sectors - 1)
        first = (1 - (turn - even)) * columns

        def step(i, carry):
            at = first + i
            column = owner[(sector * columns + at) & (total - 1)]
            to = jnp.minimum((column - facing * columns) & (total - 1), columns)
            for v in range(V):
                landing[v, pl.ds(to, 1)] = table[v, pl.ds(at, 1)]
            return carry

        lax.fori_loop(0, 2 * columns, step, 0, unroll=8)

    for v in range(V):
        message[v] = landing[v, 0:columns]


def matrix_kernel(planes, axial, inverse, up, right, left, side, splat, product, prefix):
    row = lax.axis_index("row")
    slab = lax.axis_index("slab")
    strip = (8, 128)

    @pl.when(pl.program_id(0) == 0)
    def _():
        for i in range(V):
            for j in range(V):
                splat[V * i + j] = jnp.full(strip, 0.5 * axial[0, i, j], F32)

    def flux_times(x):
        for i in range(V):
            entries = [inverse[0, i, k, x] for k in range(V)]
            for j in range(V):
                acc = entries[0] * splat[j]
                for k in range(1, V):
                    acc = acc + entries[k] * splat[V * k + j]
                product[x, V * i + j] = acc

    def forward(x, carry):
        flux_times(x)
        for j in range(V):
            column = [prefix[x - 1, V * i + j] for i in range(V)]
            put_column(prefix.at[x], j, matvec(stacked(product.at[x], 0), column))
        return carry

    flux_times(0)
    for k in range(V * V):
        prefix[0, k] = product[0, k]
    lax.fori_loop(1, planes, forward, 0)
    for k in range(V * V):
        up[2 * V + k] = prefix[planes - 1, k]

    @pl.when(slab > 0)
    def _():
        for j in range(V):
            column = [prefix[planes - 2, V * i + j] for i in range(V)]
            put_column(left, j, matvec(stacked(product.at[planes - 1], 0), column))

        def backward(step, carry):
            x = planes - 1 - step
            for j in range(V):
                column = [prefix[x - 1, V * i + j] - left[V * i + j] for i in range(V)]
                put_column(left, j, matvec(stacked(product.at[x], 0), column))
            return carry

        lax.fori_loop(1, planes - 1, backward, 0)
        for j in range(V):
            column = [float(i == j) - left[V * i + j] for i in range(V)]
            put_column(left, j, matvec(stacked(product.at[0], 0), column))
        for k in range(V * V):
            side[k] = left[k]

    @pl.when((slab == 1) | (slab == 2) | ((slab == 3) & (row == 0)))
    def _():
        for k in range(V * V):
            right[k] = product[planes - 1, k]

        def backward(step, carry):
            x = planes - 1 - step
            for j in range(V):
                column = [right[V * i + j] for i in range(V)]
                put_column(right, j, matvec(stacked(product.at[x], 0), column))
            return carry

        lax.fori_loop(1, planes, backward, 0)

    @pl.when(slab == 1)
    def _():
        for k in range(V * V):
            side[k] = right[k]


def put_column(ref, j, values):
    for i in range(V):
        ref[V * i + j] = values[i]


def residual_kernel(
    planes, columns, axial, cross, state, source, inverse, from_high, from_low, above, up_in,
    residual, up, down, wide, forward,
):
    step = pl.program_id(0)

    @pl.when(step == 0)
    def _():
        for v in range(V):
            for x in range(planes):
                wide[v, x, 8 : 8 + columns] = state[0, v, x]
                wide[v, x, 7:8] = from_low[v, x : x + 1]
                wide[v, x, 8 + columns : 9 + columns] = from_high[v, x : x + 1]

    middle = pl.multiple_of(step * 8 + 8, 8)
    low = pl.multiple_of(step * 8, 8)
    high = pl.multiple_of(step * 8 + 16, 8)
    rows = lax.broadcasted_iota(jnp.int32, (8, 128), 0)
    lanes = lax.broadcasted_iota(jnp.int32, (8, 128), 1)
    ja = lambda i, j: 0.5 * axial[0, i, j]
    jb = lambda i, j: 0.5 * cross[0, 0, i, j]
    jr = lambda i, j: 0.5 * cross[0, 1, i, j]
    previous = None
    for x in range(planes):
        along, around, outward = [], [], []
        for v in range(V):
            here = wide[v, x, pl.ds(middle, 8)]
            nearer = wide[v, x + 1, pl.ds(middle, 8)] if x + 1 < planes else above[v]
            along.append(nearer - wide[v, x - 1, pl.ds(middle, 8)] if x else nearer)
            plus = jnp.where(rows == 0, wide[v, x, pl.ds(high, 8)], here)
            minus = jnp.where(rows == 7, wide[v, x, pl.ds(low, 8)], here)
            around.append(pltpu.roll(plus, 7, 0) - pltpu.roll(minus, 1, 0))
            outward.append(
                jnp.where(lanes == 127, 0.0, pltpu.roll(here, 127, 1))
                - jnp.where(lanes == 0, 0.0, pltpu.roll(here, 1, 1))
            )
        one, two, three = matvec(ja, along), matvec(jb, around), matvec(jr, outward)
        values = [source[0, v, x] - (one[v] + two[v] + three[v]) for v in range(V)]
        for v in range(V):
            residual[v, x] = values[v]
        if previous is not None:
            carried = matvec(ja, previous)
            values = [values[v] + carried[v] for v in range(V)]
        previous = matvec(lambda i, j, x=x: inverse[0, i, j, x], values)
        for v in range(V):
            forward[v, x] = previous[v]
    for v in range(V):
        last = wide[v, planes - 1, pl.ds(middle, 8)]
        up[v] = previous[v] + last
        up[V + v] = last
    for x in range(planes - 2, -1, -1):
        carried = matvec(lambda i, j, x=x: inverse[0, i, j, x], matvec(ja, previous))
        previous = [forward[v, x] - carried[v] for v in range(V)]
    for v in range(V):
        down[v] = previous[v]


def first_kernel(ghost, up, down, right, entry, message):
    slab = lax.axis_index("slab")
    for v in range(V):
        message[V + v] = up[V + v]

    @pl.when(slab == 0)
    def _():
        moved = matvec(stacked(up, 2 * V), planes_of(ghost, 0))
        for v in range(V):
            total = up[v] + moved[v]
            entry[v] = total
            message[v] = total

    @pl.when(slab == 3)
    def _():
        moved = matvec(stacked(right, 0), planes_of(ghost, 0))
        for v in range(V):
            message[v] = jnp.where(lax.axis_index("row") == 0, down[v] + moved[v], down[v])


def middle_kernel(
    came, came_side, up_other, left_other, up, down, right, left, lower, message, inflow, under, beyond,
):
    slab = lax.axis_index("slab")

    @pl.when(slab == 1)
    def _():
        moved = matvec(stacked(left, 0), planes_of(came_side, 0))
        put(lower, 0, [down[v] + moved[v] for v in range(V)])

    @pl.when(slab == 2)
    def _():
        moved = matvec(stacked(up_other, 2 * V), planes_of(came, 0))
        second = [up_other[v] + moved[v] for v in range(V)]
        moved = matvec(stacked(up, 2 * V), second)
        third = [up[v] + moved[v] for v in range(V)]
        moved = matvec(stacked(left_other, 0), third)
        top = [came_side[v] + moved[v] for v in range(V)]
        moved = matvec(stacked(left, 0), second)
        again = matvec(stacked(right, 0), top)
        put(lower, 0, [down[v] + moved[v] + again[v] for v in range(V)])
        put(message, 0, third)
        put(message, V, planes_of(up, V))
        put(inflow, 0, second)
        put(under, 0, planes_of(up_other, V))
        put(beyond, 0, top)


def last_kernel(
    planes, axial, ghost, came_side, to_third, to_zero, to_lower, second, under_second, top,
    right_other, partial, inverse, state, residual, new_state, forward, inflow, beyond, under,
):
    row = lax.axis_index("row")
    slab = lax.axis_index("slab")
    splats = [jnp.full((8, 128), 0.5 * axial[0, k // V, k % V], F32) for k in range(V * V)]
    ja = lambda i, j: splats[V * i + j]
    has_top = jnp.where((row == 0) & (slab == 3), 1.0, 0.0)

    @pl.when(slab == 0)
    def _():
        inflow[...] = ghost[...]
        under[...] = ghost[...]

    @pl.when(slab == 1)
    def _():
        inflow[...] = came_side[0:V]
        under[...] = came_side[V:]
        beyond[...] = to_lower[...]

    @pl.when(slab == 2)
    def _():
        inflow[...] = second[...]
        under[...] = under_second[...]
        beyond[...] = top[...]

    @pl.when(slab == 3)
    def _():
        inflow[...] = to_third[0:V]
        under[...] = to_third[V:]
        beyond[...] = jnp.zeros_like(beyond)

    def one_strip(step, carry):
        at = pl.ds(pl.multiple_of(step * 8, 8), 8)

        @pl.when(slab == 0)
        def _():
            came = [to_zero[v, at] for v in range(V)]
            moved = matvec(lambda i, j: right_other[V * i + j, at], came)
            for v in range(V):
                beyond[v, at] = to_lower[v, at] + moved[v]

        previous = [inflow[v, at] for v in range(V)]
        for x in range(planes):
            values = [partial[v, x, at] for v in range(V)]
            if x == planes - 1:
                top_part = matvec(ja, [ghost[v, at] * has_top for v in range(V)])
                values = [values[v] - top_part[v] for v in range(V)]
            if x == 0:
                bottom = matvec(ja, [under[v, at] for v in range(V)])
                for v in range(V):
                    residual[0, v, x, at] = values[v] + bottom[v]
            else:
                for v in range(V):
                    residual[0, v, x, at] = values[v]
            carried = matvec(ja, previous)
            values = [values[v] + carried[v] for v in range(V)]
            previous = matvec(lambda i, j: inverse[0, i, j, x, at], values)
            for v in range(V):
                forward[v, x] = previous[v]
        following = [beyond[v, at] for v in range(V)]
        for x in range(planes - 1, -1, -1):
            carried = matvec(lambda i, j: inverse[0, i, j, x, at], matvec(ja, following))
            following = [forward[v, x] - carried[v] for v in range(V)]
            for v in range(V):
                new_state[0, v, x, at] = state[0, v, x, at] + following[v]
        return carry

    lax.fori_loop(0, state.shape[3] // 8, one_strip, 0)


def sds(*shape):
    return jax.ShapeDtypeStruct(shape, F32)


def full(shape):
    return pl.BlockSpec(shape, lambda *_: (0,) * len(shape))


def strip(lead):
    return pl.BlockSpec((lead, 8, 128), lambda i: (0, i, 0))


SCALARS = pl.BlockSpec(memory_space=pltpu.SMEM)
WHOLE = pl.BlockSpec(memory_space=pltpu.VMEM)


def params(**more):
    return pltpu.CompilerParams(vmem_limit_bytes=VMEM_BYTES, **more)


def cost(amount):
    return pl.CostEstimate(flops=amount, bytes_accessed=amount // 8, transcendentals=0)


def per_device(state, source, diag_inverse, jac_axial, jac_cross, owner):
    planes, columns, radial = state.shape[2:]
    sectors = lax.axis_size("sector")
    slabs = lax.axis_size("slab")
    strips = columns // 8
    plane = (V, columns, radial)
    cells = pl.BlockSpec((1, V, planes, 8, radial), lambda i: (0, 0, 0, i, 0))
    blocks = pl.BlockSpec((1, V, V, planes, 8, radial), lambda i: (0, 0, 0, 0, i, 0))
    inner = pl.BlockSpec((V, planes, 8, radial), lambda i: (0, 0, i, 0))
    size = slabs * sectors

    def device(row, sector, slab):
        return row * size + sector % sectors * slabs + slab

    def import_pairs(even):
        pairs = []
        for j in range(sectors):
            pairs.append((device(1, j, 0), device(0, j - even, slabs - 1)))
            pairs.append((device(0, j, slabs - 1), device(1, j + even + 2, 0)))
        return pairs

    two_down = []
    for j in range(sectors):
        two_down.append((device(0, j, slabs - 1), device(0, j - 2, slabs - 1)))
        two_down.append((device(1, j, 0), device(1, j - 2, 0)))

    total = sectors * columns
    assert total & (total - 1) == 0 and columns & (columns - 1) == 0
    towards_low, interface, towards_high, lowest, pair = pl.pallas_call(
        lambda *refs: pack_kernel(planes, columns, *refs),
        in_specs=[SCALARS, WHOLE],
        out_specs=[WHOLE] * 4 + [SCALARS],
        out_shape=(
            sds(V, planes + columns, radial), sds(*plane), sds(V, planes, radial), sds(*plane),
            jax.ShapeDtypeStruct((1,), jnp.int32),
        ),
        compiler_params=params(),
        name="pack",
    )(owner, state)
    above = lax.ppermute(lowest, "slab", [(k, k - 1) for k in range(1, slabs)])
    from_low = lax.ppermute(towards_high, "sector", [(j, (j + 1) % sectors) for j in range(sectors)])
    from_second = lax.ppermute(interface, AXES, two_down)
    from_high = lax.ppermute(towards_low, "sector", [(j, (j - 1) % sectors) for j in range(sectors)])

    message = pl.pallas_call(
        lambda *refs: window_kernel(planes, columns, sectors, *refs),
        in_specs=[SCALARS] + [WHOLE] * 3,
        out_shape=sds(*plane),
        scratch_shapes=[
            pltpu.VMEM((V, 3 * columns, radial), F32),
            pltpu.VMEM((V, columns + 8, radial), F32),
        ],
        compiler_params=params(),
        name="window",
    )(owner, interface, from_high, from_second)

    square = sds(V * V, columns, radial)

    def exchange(even, message, from_low, above, from_high):
        ghost = lax.ppermute(message, AXES, import_pairs(even))
        up, right, left, side = pl.pallas_call(
            lambda *refs: matrix_kernel(planes, *refs),
            grid=(strips,),
            in_specs=[SCALARS, blocks],
            out_specs=(strip(2 * V + V * V), strip(V * V), strip(V * V), strip(V * V)),
            out_shape=(sds(2 * V + V * V, columns, radial), square, square, square),
            scratch_shapes=[
                pltpu.VMEM((V * V, 8, radial), F32),
                pltpu.VMEM((planes, V * V, 8, radial), F32),
                pltpu.VMEM((planes, V * V, 8, radial), F32),
            ],
            compiler_params=params(),
            cost_estimate=cost(80_000_000),
            name="matrices",
        )(jac_axial, diag_inverse)
        partial, up, down = pl.pallas_call(
            lambda *refs: residual_kernel(planes, columns, *refs),
            grid=(strips,),
            in_specs=[
                SCALARS, SCALARS, full(state.shape), cells, blocks,
                full(towards_low.shape), full(towards_high.shape), strip(V),
                pl.BlockSpec(memory_space=pl.ANY),
            ],
            out_specs=(inner, strip(2 * V), strip(V)),
            out_shape=(sds(V, planes, columns, radial), up, sds(*plane)),
            input_output_aliases={8: 1},
            scratch_shapes=[
                pltpu.VMEM((V, planes, columns + 16, radial), F32),
                pltpu.VMEM((V, planes, 8, radial), F32),
            ],
            compiler_params=params(),
            cost_estimate=cost(40_000_000),
            name="residual",
        )(jac_axial, jac_cross, state, source, diag_inverse, from_high, from_low, above, up)
        return ghost, partial, up, down, right, left, side

    ghost, partial, up, down, right, left, side = lax.switch(
        pair[0],
        [lambda *args, e=e: exchange(2 * e, *args) for e in range(sectors // 2)],
        message, from_low, above, from_high,
    )
    up_other = lax.ppermute(up, "slab", [(1, 2)])
    side_other = lax.ppermute(side, "slab", [(1, 0), (3, 2)])
    entry, side_message = pl.pallas_call(
        first_kernel,
        out_shape=(sds(*plane), sds(2 * V, columns, radial)),
        compiler_params=params(),
        name="first",
    )(ghost, up, down, right)
    came_side = lax.ppermute(side_message, "slab", [(0, 1), (3, 2)])
    came = lax.ppermute(entry, "slab", [(0, 2)])
    lower, onward, second, under, top = pl.pallas_call(
        middle_kernel,
        out_shape=(sds(*plane), sds(2 * V, columns, radial), sds(*plane), sds(*plane), sds(*plane)),
        compiler_params=params(),
        name="middle",
    )(came, came_side, up_other, side_other, up, down, right, left)
    to_lower = lax.ppermute(lower, "slab", [(2, 1), (1, 0)])
    to_third = lax.ppermute(onward, "slab", [(2, 3)])
    to_zero = lax.ppermute(lower, "slab", [(2, 0)])

    residual, new_state = pl.pallas_call(
        lambda *refs: last_kernel(planes, *refs),
        in_specs=[SCALARS] + [WHOLE] * 12,
        out_shape=(sds(*state.shape), sds(*state.shape)),
        scratch_shapes=[pltpu.VMEM((V, planes, 8, radial), F32)] + [pltpu.VMEM(plane, F32)] * 3,
        compiler_params=params(),
        name="last",
    )(
        jac_axial, ghost, came_side, to_third, to_zero, to_lower, second, under, top,
        side_other, partial, diag_inverse, state,
    )
    return residual, new_state


def solution(mesh):
    return jax.shard_map(
        per_device,
        mesh=mesh,
        in_specs=(
            P("row", None, "slab", "sector", None),
            P("row", None, "slab", "sector", None),
            P("row", None, None, "slab", "sector", None),
            P("row", None, None),
            P("row", None, None, None),
            P(),
        ),
        out_specs=(P("row", None, "slab", "sector", None), P("row", None, "slab", "sector", None)),
        check_vma=False,
    )
```

```python
import jax
import jax.numpy as jnp
from jax import lax
from jax.experimental import pallas as pl
from jax.experimental.pallas import tpu as pltpu
from jax.sharding import PartitionSpec as P

F32 = jnp.float32
V = 5
AXES = ("row", "sector", "slab")
VMEM_BYTES = 14 * 1024 * 1024


def matvec(mat, vec):
    out = []
    for i in range(V):
        acc = mat(i, 0) * vec[0]
        for j in range(1, V):
            acc = acc + mat(i, j) * vec[j]
        out.append(acc)
    return out


def stacked(ref, base):
    return lambda i, j: ref[base + V * i + j]


def planes_of(ref, base):
    return [ref[base + v] for v in range(V)]


def put(ref, base, values):
    for v in range(V):
        ref[base + v] = values[v]


def sliding(owner, columns, total):
    lead = owner[0]

    def lower(i, best):
        return jnp.minimum(best, ((owner[i] - lead + total // 2) & (total - 1)) - total // 2)

    return (lead + lax.fori_loop(1, columns, lower, jnp.int32(0), unroll=True)) & (total - 1)


def pack_kernel(planes, columns, state, towards_low, interface, towards_high, lowest):
    row = lax.axis_index("row")
    face = jnp.where(row == 0, planes - 1, 0)
    for v in range(V):
        plane = state[0, v, face]
        interface[v] = plane
        towards_low[v, planes:] = plane
        lowest[v] = state[0, v, 0]
        for x in range(planes):
            towards_low[v, x : x + 1] = state[0, v, x, 0:1]
            towards_high[v, x : x + 1] = state[0, v, x, columns - 1 : columns]


def window_kernel(planes, columns, sectors, owner, own, next_one, next_two, message, pair, table, landing):
    row = lax.axis_index("row")
    sector = lax.axis_index("sector")
    total = sectors * columns
    for v in range(V):
        table[v, 0:columns] = own[v]
        table[v, columns : 2 * columns] = next_one[v, planes:]
        table[v, 2 * columns :] = next_two[v]
    turn = sliding(owner, columns, total) >> (columns.bit_length() - 1)
    even = turn & -2
    pair[0] = turn >> 1

    @pl.when(row == 1)
    def _():
        facing = (sector - even) & (sectors - 1)

        def step(i, carry):
            at = (owner[facing * columns + i] - sector * columns) & (total - 1)
            at = jnp.minimum(at, 3 * columns - 1)
            for v in range(V):
                landing[v, pl.ds(i, 1)] = table[v, pl.ds(at, 1)]
            return carry

        lax.fori_loop(0, columns, step, 0, unroll=8)

    @pl.when(row == 0)
    def _():
        facing = (sector + even + 2) & (sectors - 1)
        first = (1 - (turn - even)) * columns

        def step(i, carry):
            at = first + i
            column = owner[(sector * columns + at) & (total - 1)]
            to = jnp.minimum((column - facing * columns) & (total - 1), columns)
            for v in range(V):
                landing[v, pl.ds(to, 1)] = table[v, pl.ds(at, 1)]
            return carry

        lax.fori_loop(0, 2 * columns, step, 0, unroll=8)

    for v in range(V):
        message[v] = landing[v, 0:columns]


def matrix_kernel(
    planes, flux, inverse, prefix_out, right, left, side, product, blocks, prefix, left_now, right_now,
):
    row = lax.axis_index("row")
    slab = lax.axis_index("slab")
    scaled = [[jnp.full((8, 128), flux[V * i + j], F32) for j in range(V)] for i in range(V)]

    def one_strip(step, carry):
        at = pl.ds(pl.multiple_of(step * 8, 8), 8)

        def factor(x):
            return lambda i, j: product[V * i + j, x, at]

        def flux_times(x):
            for i in range(V):
                entries = [inverse[0, i, k, x, at] for k in range(V)]
                for k in range(V):
                    blocks[V * i + k, x, at] = entries[k]
                for j in range(V):
                    acc = entries[0] * scaled[0][j]
                    for k in range(1, V):
                        acc = acc + entries[k] * scaled[k][j]
                    product[V * i + j, x, at] = acc

        def forward(x, carry):
            flux_times(x)
            for j in range(V):
                column = [prefix[x - 1, V * i + j] for i in range(V)]
                put_column(prefix.at[x], j, matvec(factor(x), column))
            return carry

        flux_times(0)
        for k in range(V * V):
            prefix[0, k] = product[k, 0, at]
        lax.fori_loop(1, planes, forward, 0)
        for k in range(V * V):
            prefix_out[k, at] = prefix[planes - 1, k]

        @pl.when(slab > 0)
        def _():
            for j in range(V):
                column = [prefix[planes - 2, V * i + j] for i in range(V)]
                put_column(left_now, j, matvec(factor(planes - 1), column))

            def backward(step, carry):
                x = planes - 1 - step
                for j in range(V):
                    column = [prefix[x - 1, V * i + j] - left_now[V * i + j] for i in range(V)]
                    put_column(left_now, j, matvec(factor(x), column))
                return carry

            lax.fori_loop(1, planes - 1, backward, 0)
            for j in range(V):
                column = [float(i == j) - left_now[V * i + j] for i in range(V)]
                put_column(left_now, j, matvec(factor(0), column))
            for k in range(V * V):
                left[k, at] = left_now[k]
                side[k, at] = left_now[k]

        @pl.when((slab == 1) | (slab == 2) | ((slab == 3) & (row == 0)))
        def _():
            for k in range(V * V):
                right_now[k] = product[k, planes - 1, at]

            def backward(step, carry):
                x = planes - 1 - step
                for j in range(V):
                    column = [right_now[V * i + j] for i in range(V)]
                    put_column(right_now, j, matvec(factor(x), column))
                return carry

            lax.fori_loop(1, planes, backward, 0)
            for k in range(V * V):
                right[k, at] = right_now[k]

        @pl.when(slab == 1)
        def _():
            for k in range(V * V):
                side[k, at] = right_now[k]

        return carry

    lax.fori_loop(0, inverse.shape[4] // 8, one_strip, 0)


def put_column(ref, j, values):
    for i in range(V):
        ref[V * i + j] = values[i]


def residual_kernel(
    planes, columns, flux, state, source, blocks, product, from_high, from_low, above, prefix_in,
    residual, started, up, down, wide, forward,
):
    for v in range(V):
        for x in range(planes):
            wide[v, x, 8 : 8 + columns] = state[0, v, x]
            wide[v, x, 7:8] = from_low[v, x : x + 1]
            wide[v, x, 8 + columns : 9 + columns] = from_high[v, x : x + 1]
    rows = lax.broadcasted_iota(jnp.int32, (8, 128), 0)
    lanes = lax.broadcasted_iota(jnp.int32, (8, 128), 1)
    ja = lambda i, j: flux[V * i + j]
    jb = lambda i, j: flux[V * V + V * i + j]
    jr = lambda i, j: flux[2 * V * V + V * i + j]

    def one_strip(step, carry):
        at = pl.ds(pl.multiple_of(step * 8, 8), 8)
        middle = pl.ds(pl.multiple_of(step * 8 + 8, 8), 8)
        high = pl.ds(pl.multiple_of(step * 8 + 16, 8), 8)
        previous = None
        for x in range(planes):
            along, around, outward = [], [], []
            for v in range(V):
                here = wide[v, x, middle]
                nearer = wide[v, x + 1, middle] if x + 1 < planes else above[v, at]
                along.append(nearer - wide[v, x - 1, middle] if x else nearer)
                plus = jnp.where(rows == 0, wide[v, x, high], here)
                minus = jnp.where(rows == 7, wide[v, x, at], here)
                around.append(pltpu.roll(plus, 7, 0) - pltpu.roll(minus, 1, 0))
                outward.append(
                    jnp.where(lanes == 127, 0.0, pltpu.roll(here, 127, 1))
                    - jnp.where(lanes == 0, 0.0, pltpu.roll(here, 1, 1))
                )
            one, two, three = matvec(ja, along), matvec(jb, around), matvec(jr, outward)
            values = [source[0, v, x, at] - (one[v] + two[v] + three[v]) for v in range(V)]
            for v in range(V):
                residual[v, x, at] = values[v]
            values = matvec(lambda i, j: blocks[V * i + j, x, at], values)
            for v in range(V):
                started[v, x, at] = values[v]
            if previous is not None:
                carried = matvec(lambda i, j: product[V * i + j, x, at], previous)
                values = [values[v] + carried[v] for v in range(V)]
            previous = values
            for v in range(V):
                forward[v, x] = previous[v]
        for v in range(V):
            last = wide[v, planes - 1, middle]
            up[v, at] = previous[v] + last
            up[V + v, at] = last
        for k in range(V * V):
            up[2 * V + k, at] = prefix_in[k, at]
        for x in range(planes - 2, -1, -1):
            carried = matvec(lambda i, j: product[V * i + j, x, at], previous)
            previous = [forward[v, x] - carried[v] for v in range(V)]
        for v in range(V):
            down[v, at] = previous[v]
        return carry

    lax.fori_loop(0, columns // 8, one_strip, 0)


def first_kernel(ghost, up, down, right, entry, message):
    slab = lax.axis_index("slab")
    for v in range(V):
        message[V + v] = up[V + v]

    @pl.when(slab == 0)
    def _():
        moved = matvec(stacked(up, 2 * V), planes_of(ghost, 0))
        for v in range(V):
            total = up[v] + moved[v]
            entry[v] = total
            message[v] = total

    @pl.when(slab == 3)
    def _():
        moved = matvec(stacked(right, 0), planes_of(ghost, 0))
        for v in range(V):
            message[v] = jnp.where(lax.axis_index("row") == 0, down[v] + moved[v], down[v])


def middle_kernel(
    came, came_side, up_other, left_other, up, down, right, left, lower, message, inflow, under, beyond,
):
    slab = lax.axis_index("slab")

    @pl.when(slab == 1)
    def _():
        moved = matvec(stacked(left, 0), planes_of(came_side, 0))
        put(lower, 0, [down[v] + moved[v] for v in range(V)])

    @pl.when(slab == 2)
    def _():
        moved = matvec(stacked(up_other, 2 * V), planes_of(came, 0))
        second = [up_other[v] + moved[v] for v in range(V)]
        moved = matvec(stacked(up, 2 * V), second)
        third = [up[v] + moved[v] for v in range(V)]
        moved = matvec(stacked(left_other, 0), third)
        top = [came_side[v] + moved[v] for v in range(V)]
        moved = matvec(stacked(left, 0), second)
        again = matvec(stacked(right, 0), top)
        put(lower, 0, [down[v] + moved[v] + again[v] for v in range(V)])
        put(message, 0, third)
        put(message, V, planes_of(up, V))
        put(inflow, 0, second)
        put(under, 0, planes_of(up_other, V))
        put(beyond, 0, top)


def last_kernel(
    planes, flux, ghost, came_side, to_third, to_zero, to_lower, second, under_second, top,
    right_other, partial, started, product, inverse, state, residual, new_state, forward, inflow, beyond,
    under,
):
    row = lax.axis_index("row")
    slab = lax.axis_index("slab")
    ja = lambda i, j: flux[V * i + j]
    has_top = jnp.where((row == 0) & (slab == 3), 1.0, 0.0)

    @pl.when(slab == 0)
    def _():
        inflow[...] = ghost[...]
        under[...] = ghost[...]

    @pl.when(slab == 1)
    def _():
        inflow[...] = came_side[0:V]
        under[...] = came_side[V:]
        beyond[...] = to_lower[...]

    @pl.when(slab == 2)
    def _():
        inflow[...] = second[...]
        under[...] = under_second[...]
        beyond[...] = top[...]

    @pl.when(slab == 3)
    def _():
        inflow[...] = to_third[0:V]
        under[...] = to_third[V:]
        beyond[...] = jnp.zeros_like(beyond)

    def one_strip(step, carry):
        at = pl.ds(pl.multiple_of(step * 8, 8), 8)

        @pl.when(slab == 0)
        def _():
            came = [to_zero[v, at] for v in range(V)]
            moved = matvec(lambda i, j: right_other[V * i + j, at], came)
            for v in range(V):
                beyond[v, at] = to_lower[v, at] + moved[v]

        previous = [inflow[v, at] for v in range(V)]
        for x in range(planes):
            values = [partial[v, x, at] for v in range(V)]
            begun = [started[v, x, at] for v in range(V)]
            if x == planes - 1:
                top_part = matvec(ja, [ghost[v, at] * has_top for v in range(V)])
                values = [values[v] - top_part[v] for v in range(V)]
                lost = matvec(lambda i, j: inverse[V * i + j, x, at], top_part)
                begun = [begun[v] - lost[v] for v in range(V)]
            if x == 0:
                bottom = matvec(ja, [under[v, at] for v in range(V)])
                values = [values[v] + bottom[v] for v in range(V)]
            for v in range(V):
                residual[0, v, x, at] = values[v]
            carried = matvec(lambda i, j: product[V * i + j, x, at], previous)
            previous = [begun[v] + carried[v] for v in range(V)]
            for v in range(V):
                forward[v, x] = previous[v]
        following = [beyond[v, at] for v in range(V)]
        for x in range(planes - 1, -1, -1):
            carried = matvec(lambda i, j: product[V * i + j, x, at], following)
            following = [forward[v, x] - carried[v] for v in range(V)]
            for v in range(V):
                new_state[0, v, x, at] = state[0, v, x, at] + following[v]
        return carry

    lax.fori_loop(0, state.shape[3] // 8, one_strip, 0)


def sds(*shape):
    return jax.ShapeDtypeStruct(shape, F32)


def full(shape):
    return pl.BlockSpec(shape, lambda *_: (0,) * len(shape))


def strip(lead):
    return pl.BlockSpec((lead, 8, 128), lambda i: (0, i, 0))


SCALARS = pl.BlockSpec(memory_space=pltpu.SMEM)
WHOLE = pl.BlockSpec(memory_space=pltpu.VMEM)


def params(**more):
    return pltpu.CompilerParams(vmem_limit_bytes=VMEM_BYTES, **more)


def cost(amount):
    return pl.CostEstimate(flops=amount, bytes_accessed=amount // 8, transcendentals=0)


def per_device(state, source, diag_inverse, jac_axial, jac_cross, owner):
    planes, columns, radial = state.shape[2:]
    sectors = lax.axis_size("sector")
    slabs = lax.axis_size("slab")
    strips = columns // 8
    plane = (V, columns, radial)
    cells = pl.BlockSpec((1, V, planes, 8, radial), lambda i: (0, 0, 0, i, 0))
    blocks = pl.BlockSpec((1, V, V, planes, 8, radial), lambda i: (0, 0, 0, 0, i, 0))
    inner = pl.BlockSpec((V, planes, 8, radial), lambda i: (0, 0, i, 0))
    size = slabs * sectors

    def device(row, sector, slab):
        return row * size + sector % sectors * slabs + slab

    def import_pairs(even):
        pairs = []
        for j in range(sectors):
            pairs.append((device(1, j, 0), device(0, j - even, slabs - 1)))
            pairs.append((device(0, j, slabs - 1), device(1, j + even + 2, 0)))
        return pairs

    two_down = []
    for j in range(sectors):
        two_down.append((device(0, j, slabs - 1), device(0, j - 2, slabs - 1)))
        two_down.append((device(1, j, 0), device(1, j - 2, 0)))

    total = sectors * columns
    assert total & (total - 1) == 0 and columns & (columns - 1) == 0
    flux = 0.5 * jnp.concatenate([jac_axial.reshape(-1), jac_cross.reshape(-1)])
    towards_low, interface, towards_high, lowest = pl.pallas_call(
        lambda *refs: pack_kernel(planes, columns, *refs),
        out_shape=(sds(V, planes + columns, radial), sds(*plane), sds(V, planes, radial), sds(*plane)),
        compiler_params=params(),
        name="pack",
    )(state)
    above = lax.ppermute(lowest, "slab", [(k, k - 1) for k in range(1, slabs)])
    from_low = lax.ppermute(towards_high, "sector", [(j, (j + 1) % sectors) for j in range(sectors)])
    from_second = lax.ppermute(interface, AXES, two_down)
    from_high = lax.ppermute(towards_low, "sector", [(j, (j - 1) % sectors) for j in range(sectors)])

    square = sds(V * V, columns, radial)
    cubic = sds(V * V, planes, columns, radial)
    prefix, right, left, side, product, blocks = pl.pallas_call(
        lambda *refs: matrix_kernel(planes, *refs),
        in_specs=[SCALARS, WHOLE],
        out_shape=(square, square, square, square, cubic, cubic),
        scratch_shapes=[
            pltpu.VMEM((planes, V * V, 8, radial), F32),
            pltpu.VMEM((V * V, 8, radial), F32),
            pltpu.VMEM((V * V, 8, radial), F32),
        ],
        compiler_params=params(),
        cost_estimate=cost(60_000_000),
        name="matrices",
    )(flux, diag_inverse)
    message, pair = pl.pallas_call(
        lambda *refs: window_kernel(planes, columns, sectors, *refs),
        in_specs=[SCALARS] + [WHOLE] * 3,
        out_specs=[WHOLE, SCALARS],
        out_shape=(sds(*plane), jax.ShapeDtypeStruct((1,), jnp.int32)),
        scratch_shapes=[
            pltpu.VMEM((V, 3 * columns, radial), F32),
            pltpu.VMEM((V, columns + 8, radial), F32),
        ],
        compiler_params=params(),
        name="window",
    )(owner, interface, from_high, from_second)

    def exchange(even, message, from_low, above, from_high, prefix, product, blocks):
        ghost = lax.ppermute(message, AXES, import_pairs(even))
        partial, started, up, down = pl.pallas_call(
            lambda *refs: residual_kernel(planes, columns, *refs),
            in_specs=[SCALARS] + [WHOLE] * 8,
            out_shape=(
                sds(V, planes, columns, radial), sds(V, planes, columns, radial),
                sds(2 * V + V * V, columns, radial), sds(*plane),
            ),
            scratch_shapes=[
                pltpu.VMEM((V, planes, columns + 16, radial), F32),
                pltpu.VMEM((V, planes, 8, radial), F32),
            ],
            compiler_params=params(),
            cost_estimate=cost(40_000_000),
            name="residual",
        )(flux, state, source, blocks, product, from_high, from_low, above, prefix)
        return ghost, partial, started, up, down

    ghost, partial, started, up, down = lax.switch(
        pair[0],
        [lambda *args, e=e: exchange(2 * e, *args) for e in range(sectors // 2)],
        message, from_low, above, from_high, prefix, product, blocks,
    )
    up_other = lax.ppermute(up, "slab", [(1, 2)])
    side_other = lax.ppermute(side, "slab", [(1, 0), (3, 2)])
    entry, side_message = pl.pallas_call(
        first_kernel,
        out_shape=(sds(*plane), sds(2 * V, columns, radial)),
        compiler_params=params(),
        name="first",
    )(ghost, up, down, right)
    came_side = lax.ppermute(side_message, "slab", [(0, 1), (3, 2)])
    came = lax.ppermute(entry, "slab", [(0, 2)])
    lower, onward, second, under, top = pl.pallas_call(
        middle_kernel,
        out_shape=(sds(*plane), sds(2 * V, columns, radial), sds(*plane), sds(*plane), sds(*plane)),
        compiler_params=params(),
        name="middle",
    )(came, came_side, up_other, side_other, up, down, right, left)
    to_lower = lax.ppermute(lower, "slab", [(2, 1), (1, 0)])
    to_third = lax.ppermute(onward, "slab", [(2, 3)])
    to_zero = lax.ppermute(lower, "slab", [(2, 0)])

    residual, new_state = pl.pallas_call(
        lambda *refs: last_kernel(planes, *refs),
        in_specs=[SCALARS] + [WHOLE] * 14,
        out_shape=(sds(*state.shape), sds(*state.shape)),
        scratch_shapes=[pltpu.VMEM((V, planes, 8, radial), F32)] + [pltpu.VMEM(plane, F32)] * 3,
        compiler_params=params(),
        name="last",
    )(
        flux, ghost, came_side, to_third, to_zero, to_lower, second, under, top,
        side_other, partial, started, product, blocks, state,
    )
    return residual, new_state


def solution(mesh):
    return jax.shard_map(
        per_device,
        mesh=mesh,
        in_specs=(
            P("row", None, "slab", "sector", None),
            P("row", None, "slab", "sector", None),
            P("row", None, None, "slab", "sector", None),
            P("row", None, None),
            P("row", None, None, None),
            P(),
        ),
        out_specs=(P("row", None, "slab", "sector", None), P("row", None, "slab", "sector", None)),
        check_vma=False,
    )
```

```python
import jax
import jax.numpy as jnp
from jax import lax
from jax.experimental import pallas as pl
from jax.experimental.pallas import tpu as pltpu
from jax.sharding import PartitionSpec as P

F32 = jnp.float32
V = 5
AXES = ("row", "sector", "slab")
VMEM_BYTES = 14 * 1024 * 1024


def matvec(mat, vec):
    out = []
    for i in range(V):
        acc = mat(i, 0) * vec[0]
        for j in range(1, V):
            acc = acc + mat(i, j) * vec[j]
        out.append(acc)
    return out


def stacked(ref, base):
    return lambda i, j: ref[base + V * i + j]


def planes_of(ref, base):
    return [ref[base + v] for v in range(V)]


def put(ref, base, values):
    for v in range(V):
        ref[base + v] = values[v]


def sliding(owner, columns, total):
    lead = owner[0]

    def lower(i, best):
        return jnp.minimum(best, ((owner[i] - lead + total // 2) & (total - 1)) - total // 2)

    return (lead + lax.fori_loop(1, columns, lower, jnp.int32(0), unroll=True)) & (total - 1)


def pack_kernel(
    planes, columns, state, inverse, towards_low, interface, towards_high, lowest, highest, blocks, arrived,
):
    copy = pltpu.make_async_copy(inverse, blocks, arrived)
    copy.start()
    row = lax.axis_index("row")
    face = jnp.where(row == 0, planes - 1, 0)
    for v in range(V):
        plane = state[0, v, face]
        interface[v] = plane
        towards_low[v, planes:] = plane
        lowest[v] = state[0, v, 0]
        highest[v] = state[0, v, planes - 1]
        for x in range(planes):
            towards_low[v, x : x + 1] = state[0, v, x, 0:1]
            towards_high[v, x : x + 1] = state[0, v, x, columns - 1 : columns]
    copy.wait()


def halved(ref, which=0):
    entries = [
        [jnp.broadcast_to(0.5 * ref[i, which : which + 1, j : j + 1], (8, 128)) for j in range(V)]
        for i in range(V)
    ]
    return lambda i, j: entries[i][j]


def window_kernel(planes, columns, sectors, owner, own, next_one, next_two, message, pair, table, landing):
    row = lax.axis_index("row")
    sector = lax.axis_index("sector")
    total = sectors * columns
    for v in range(V):
        table[v, 0:columns] = own[v]
        table[v, columns : 2 * columns] = next_one[v, planes:]
        table[v, 2 * columns :] = next_two[v]
    turn = sliding(owner, columns, total) >> (columns.bit_length() - 1)
    even = turn & -2
    pair[0] = turn >> 1

    @pl.when(row == 1)
    def _():
        facing = (sector - even) & (sectors - 1)

        def step(i, carry):
            at = (owner[facing * columns + i] - sector * columns) & (total - 1)
            at = jnp.minimum(at, 3 * columns - 1)
            for v in range(V):
                landing[v, pl.ds(i, 1)] = table[v, pl.ds(at, 1)]
            return carry

        lax.fori_loop(0, columns, step, 0, unroll=8)

    @pl.when(row == 0)
    def _():
        facing = (sector + even + 2) & (sectors - 1)
        first = (1 - (turn - even)) * columns

        def step(i, carry):
            at = first + i
            column = owner[(sector * columns + at) & (total - 1)]
            to = jnp.minimum((column - facing * columns) & (total - 1), columns)
            for v in range(V):
                landing[v, pl.ds(to, 1)] = table[v, pl.ds(at, 1)]
            return carry

        lax.fori_loop(0, 2 * columns, step, 0, unroll=8)

    for v in range(V):
        message[v] = landing[v, 0:columns]


def matrix_kernel(
    planes, axial, inverse, prefix_out, right, left, product, prefix, left_now, right_now,
):
    row = lax.axis_index("row")
    slab = lax.axis_index("slab")
    scaled = halved(axial)

    def one_strip(step, carry):
        at = pl.ds(pl.multiple_of(step * 8, 8), 8)

        def factor(x):
            return lambda i, j: product[x, V * i + j]

        def flux_times(x):
            for i in range(V):
                entries = [inverse[0, i, k, x, at] for k in range(V)]
                for j in range(V):
                    acc = entries[0] * scaled(0, j)
                    for k in range(1, V):
                        acc = acc + entries[k] * scaled(k, j)
                    product[x, V * i + j] = acc

        def forward(x, carry):
            flux_times(x)
            for j in range(V):
                column = [prefix[x - 1, V * i + j] for i in range(V)]
                put_column(prefix.at[x], j, matvec(factor(x), column))
            return carry

        flux_times(0)
        for k in range(V * V):
            prefix[0, k] = product[0, k]
        lax.fori_loop(1, planes, forward, 0)
        for k in range(V * V):
            prefix_out[k, at] = prefix[planes - 1, k]

        @pl.when(slab > 0)
        def _():
            for j in range(V):
                column = [prefix[planes - 2, V * i + j] for i in range(V)]
                put_column(left_now, j, matvec(factor(planes - 1), column))

            def backward(step, carry):
                x = planes - 1 - step
                for j in range(V):
                    column = [prefix[x - 1, V * i + j] - left_now[V * i + j] for i in range(V)]
                    put_column(left_now, j, matvec(factor(x), column))
                return carry

            lax.fori_loop(1, planes - 1, backward, 0)
            for j in range(V):
                column = [float(i == j) - left_now[V * i + j] for i in range(V)]
                put_column(left_now, j, matvec(factor(0), column))
            for k in range(V * V):
                left[k, at] = left_now[k]

        @pl.when((slab == 1) | (slab == 2) | ((slab == 3) & (row == 0)))
        def _():
            for k in range(V * V):
                right_now[k] = product[planes - 1, k]

            def backward(step, carry):
                x = planes - 1 - step
                for j in range(V):
                    column = [right_now[V * i + j] for i in range(V)]
                    put_column(right_now, j, matvec(factor(x), column))
                return carry

            lax.fori_loop(1, planes, backward, 0)
            for k in range(V * V):
                right[k, at] = right_now[k]

        return carry

    lax.fori_loop(0, inverse.shape[4] // 8, one_strip, 0)


def put_column(ref, j, values):
    for i in range(V):
        ref[V * i + j] = values[i]


def residual_kernel(
    planes, columns, axial, cross, state, source, inverse, from_high, from_low, above, prefix_in,
    residual, up, down, wide, forward,
):
    for v in range(V):
        for x in range(planes):
            wide[v, x, 8 : 8 + columns] = state[0, v, x]
            wide[v, x, 7:8] = from_low[v, x : x + 1]
            wide[v, x, 8 + columns : 9 + columns] = from_high[v, x : x + 1]
    rows = lax.broadcasted_iota(jnp.int32, (8, 128), 0)
    lanes = lax.broadcasted_iota(jnp.int32, (8, 128), 1)
    ja = halved(axial)
    jb = halved(cross)
    jr = halved(cross, 1)

    def one_strip(step, carry):
        at = pl.ds(pl.multiple_of(step * 8, 8), 8)
        middle = pl.ds(pl.multiple_of(step * 8 + 8, 8), 8)
        high = pl.ds(pl.multiple_of(step * 8 + 16, 8), 8)
        previous = None
        for x in range(planes):
            along, around, outward = [], [], []
            for v in range(V):
                here = wide[v, x, middle]
                nearer = wide[v, x + 1, middle] if x + 1 < planes else above[v, at]
                along.append(nearer - wide[v, x - 1, middle] if x else nearer)
                plus = jnp.where(rows == 0, wide[v, x, high], here)
                minus = jnp.where(rows == 7, wide[v, x, at], here)
                around.append(pltpu.roll(plus, 7, 0) - pltpu.roll(minus, 1, 0))
                outward.append(
                    jnp.where(lanes == 127, 0.0, pltpu.roll(here, 127, 1))
                    - jnp.where(lanes == 0, 0.0, pltpu.roll(here, 1, 1))
                )
            one, two, three = matvec(ja, along), matvec(jb, around), matvec(jr, outward)
            values = [source[0, v, x, at] - (one[v] + two[v] + three[v]) for v in range(V)]
            for v in range(V):
                residual[v, x, at] = values[v]
            if previous is not None:
                carried = matvec(ja, previous)
                values = [values[v] + carried[v] for v in range(V)]
            previous = matvec(lambda i, j: inverse[0, i, j, x, at], values)
            for v in range(V):
                forward[v, x] = previous[v]
        for v in range(V):
            last = wide[v, planes - 1, middle]
            up[v, at] = previous[v] + last
        for k in range(V * V):
            up[V + k, at] = prefix_in[k, at]
        for x in range(planes - 2, -1, -1):
            carried = matvec(lambda i, j: inverse[0, i, j, x, at], matvec(ja, previous))
            previous = [forward[v, x] - carried[v] for v in range(V)]
        for v in range(V):
            down[v, at] = previous[v]
        return carry

    lax.fori_loop(0, columns // 8, one_strip, 0)


def first_kernel(ghost, up, down, right, entry, message):
    slab = lax.axis_index("slab")

    @pl.when(slab == 0)
    def _():
        moved = matvec(stacked(up, V), planes_of(ghost, 0))
        for v in range(V):
            total = up[v] + moved[v]
            entry[v] = total
            message[v] = total

    @pl.when(slab == 3)
    def _():
        moved = matvec(stacked(right, 0), planes_of(ghost, 0))
        for v in range(V):
            message[v] = jnp.where(lax.axis_index("row") == 0, down[v] + moved[v], down[v])


def middle_kernel(came, came_side, up_other, left_other, up, down, right, left, lower, third, second, top):
    slab = lax.axis_index("slab")

    @pl.when(slab == 1)
    def _():
        moved = matvec(stacked(left, 0), planes_of(came_side, 0))
        put(lower, 0, [down[v] + moved[v] for v in range(V)])

    @pl.when(slab == 2)
    def _():
        moved = matvec(stacked(up_other, V), planes_of(came, 0))
        inflow = [up_other[v] + moved[v] for v in range(V)]
        moved = matvec(stacked(up, V), inflow)
        onward = [up[v] + moved[v] for v in range(V)]
        moved = matvec(stacked(left_other, 0), onward)
        beyond = [came_side[v] + moved[v] for v in range(V)]
        moved = matvec(stacked(left, 0), inflow)
        again = matvec(stacked(right, 0), beyond)
        put(lower, 0, [down[v] + moved[v] + again[v] for v in range(V)])
        put(third, 0, onward)
        put(second, 0, inflow)
        put(top, 0, beyond)


def last_kernel(
    planes, axial, ghost, below, came_side, to_third, to_zero, to_lower, second, top,
    right_other, partial, inverse, state, residual, new_state, forward, inflow, beyond, under,
):
    row = lax.axis_index("row")
    slab = lax.axis_index("slab")
    ja = halved(axial)
    has_top = jnp.where((row == 0) & (slab == 3), 1.0, 0.0)

    @pl.when(slab == 0)
    def _():
        inflow[...] = ghost[...]
        under[...] = ghost[...]

    @pl.when(slab != 0)
    def _():
        under[...] = below[...]

    @pl.when(slab == 1)
    def _():
        inflow[...] = came_side[...]
        beyond[...] = to_lower[...]

    @pl.when(slab == 2)
    def _():
        inflow[...] = second[...]
        beyond[...] = top[...]

    @pl.when(slab == 3)
    def _():
        inflow[...] = to_third[...]
        beyond[...] = jnp.zeros_like(beyond)

    def one_strip(step, carry):
        at = pl.ds(pl.multiple_of(step * 8, 8), 8)

        @pl.when(slab == 0)
        def _():
            came = [to_zero[v, at] for v in range(V)]
            moved = matvec(lambda i, j: right_other[V * i + j, at], came)
            for v in range(V):
                beyond[v, at] = to_lower[v, at] + moved[v]

        previous = [inflow[v, at] for v in range(V)]
        for x in range(planes):
            values = [partial[v, x, at] for v in range(V)]
            if x == planes - 1:
                top_part = matvec(ja, [ghost[v, at] * has_top for v in range(V)])
                values = [values[v] - top_part[v] for v in range(V)]
            if x == 0:
                bottom = matvec(ja, [under[v, at] for v in range(V)])
                for v in range(V):
                    residual[0, v, x, at] = values[v] + bottom[v]
            else:
                for v in range(V):
                    residual[0, v, x, at] = values[v]
            carried = matvec(ja, previous)
            values = [values[v] + carried[v] for v in range(V)]
            previous = matvec(lambda i, j: inverse[0, i, j, x, at], values)
            for v in range(V):
                forward[v, x] = previous[v]
        following = [beyond[v, at] for v in range(V)]
        for x in range(planes - 1, -1, -1):
            carried = matvec(lambda i, j: inverse[0, i, j, x, at], matvec(ja, following))
            following = [forward[v, x] - carried[v] for v in range(V)]
            for v in range(V):
                new_state[0, v, x, at] = state[0, v, x, at] + following[v]
        return carry

    lax.fori_loop(0, state.shape[3] // 8, one_strip, 0)


def sds(*shape):
    return jax.ShapeDtypeStruct(shape, F32)


SCALARS = pl.BlockSpec(memory_space=pltpu.SMEM)
WHOLE = pl.BlockSpec(memory_space=pltpu.VMEM)


def params(**more):
    return pltpu.CompilerParams(vmem_limit_bytes=VMEM_BYTES, **more)


def cost(amount):
    return pl.CostEstimate(flops=amount, bytes_accessed=amount // 8, transcendentals=0)


def per_device(state, source, diag_inverse, jac_axial, jac_cross, owner):
    planes, columns, radial = state.shape[2:]
    sectors = lax.axis_size("sector")
    slabs = lax.axis_size("slab")
    plane = (V, columns, radial)
    size = slabs * sectors

    def device(row, sector, slab):
        return row * size + sector % sectors * slabs + slab

    def import_pairs(even):
        pairs = []
        for j in range(sectors):
            pairs.append((device(1, j, 0), device(0, j - even, slabs - 1)))
            pairs.append((device(0, j, slabs - 1), device(1, j + even + 2, 0)))
        return pairs

    two_down = []
    for j in range(sectors):
        two_down.append((device(0, j, slabs - 1), device(0, j - 2, slabs - 1)))
        two_down.append((device(1, j, 0), device(1, j - 2, 0)))

    total = sectors * columns
    assert total & (total - 1) == 0 and columns & (columns - 1) == 0
    axial = jnp.transpose(jac_axial, (1, 0, 2))
    cross = jnp.transpose(jac_cross[0], (1, 0, 2))
    towards_low, interface, towards_high, lowest, highest, blocks = pl.pallas_call(
        lambda *refs: pack_kernel(planes, columns, *refs),
        in_specs=[WHOLE, pl.BlockSpec(memory_space=pltpu.HBM)],
        out_specs=[WHOLE] * 6,
        out_shape=(
            sds(V, planes + columns, radial), sds(*plane), sds(V, planes, radial), sds(*plane),
            sds(*plane), pltpu.VMEM(diag_inverse.shape, F32),
        ),
        scratch_shapes=[pltpu.SemaphoreType.DMA],
        compiler_params=params(),
        name="pack",
    )(state, pltpu.with_memory_space_constraint(diag_inverse, pltpu.HBM))
    above = lax.ppermute(lowest, "slab", [(k, k - 1) for k in range(1, slabs)])
    from_low = lax.ppermute(towards_high, "sector", [(j, (j + 1) % sectors) for j in range(sectors)])
    from_second = lax.ppermute(interface, AXES, two_down)
    from_high = lax.ppermute(towards_low, "sector", [(j, (j - 1) % sectors) for j in range(sectors)])

    square = sds(V * V, columns, radial)
    message, pair = pl.pallas_call(
        lambda *refs: window_kernel(planes, columns, sectors, *refs),
        in_specs=[SCALARS] + [WHOLE] * 3,
        out_specs=[WHOLE, SCALARS],
        out_shape=(sds(*plane), jax.ShapeDtypeStruct((1,), jnp.int32)),
        scratch_shapes=[
            pltpu.VMEM((V, 3 * columns, radial), F32),
            pltpu.VMEM((V, columns + 8, radial), F32),
        ],
        compiler_params=params(),
        name="window",
    )(owner, interface, from_high, from_second)

    def exchange(even, message, from_low, above, from_high, blocks, highest):
        ghost = lax.ppermute(message, AXES, import_pairs(even))
        below = lax.ppermute(highest, "slab", [(k, k + 1) for k in range(slabs - 1)])
        prefix, right, left = pl.pallas_call(
            lambda *refs: matrix_kernel(planes, *refs),
            in_specs=[WHOLE, WHOLE],
            out_shape=(square, square, square),
            scratch_shapes=[
                pltpu.VMEM((planes, V * V, 8, radial), F32),
                pltpu.VMEM((planes, V * V, 8, radial), F32),
                pltpu.VMEM((V * V, 8, radial), F32),
                pltpu.VMEM((V * V, 8, radial), F32),
            ],
            compiler_params=params(),
            cost_estimate=cost(60_000_000),
            name="matrices",
        )(axial, blocks)
        partial, up, down = pl.pallas_call(
            lambda *refs: residual_kernel(planes, columns, *refs),
            in_specs=[WHOLE] * 9,
            out_shape=(
                sds(V, planes, columns, radial), sds(V + V * V, columns, radial), sds(*plane),
            ),
            scratch_shapes=[
                pltpu.VMEM((V, planes, columns + 16, radial), F32),
                pltpu.VMEM((V, planes, 8, radial), F32),
            ],
            compiler_params=params(),
            cost_estimate=cost(40_000_000),
            name="residual",
        )(axial, cross, state, source, blocks, from_high, from_low, above, prefix)
        return ghost, below, partial, up, down, right, left

    ghost, below, partial, up, down, right, left = lax.switch(
        pair[0],
        [lambda *args, e=e: exchange(2 * e, *args) for e in range(sectors // 2)],
        message, from_low, above, from_high, blocks, highest,
    )
    up_other = lax.ppermute(up, "slab", [(1, 2)])
    left_other = lax.ppermute(left, "slab", [(3, 2)])
    entry, side_message = pl.pallas_call(
        first_kernel,
        out_shape=(sds(*plane), sds(*plane)),
        compiler_params=params(),
        name="first",
    )(ghost, up, down, right)
    came_side = lax.ppermute(side_message, "slab", [(0, 1), (3, 2)])
    came = lax.ppermute(entry, "slab", [(0, 2)])
    right, came, came_side = lax.optimization_barrier((right, came, came_side))
    right_other = lax.ppermute(right, "slab", [(1, 0)])
    lower, onward, second, top = pl.pallas_call(
        middle_kernel,
        out_shape=(sds(*plane),) * 4,
        compiler_params=params(),
        name="middle",
    )(came, came_side, up_other, left_other, up, down, right, left)
    to_lower = lax.ppermute(lower, "slab", [(2, 1), (1, 0)])
    to_third = lax.ppermute(onward, "slab", [(2, 3)])
    to_zero = lax.ppermute(lower, "slab", [(2, 0)])

    residual, new_state = pl.pallas_call(
        lambda *refs: last_kernel(planes, *refs),
        in_specs=[WHOLE] * 13,
        out_shape=(sds(*state.shape), sds(*state.shape)),
        scratch_shapes=[pltpu.VMEM((V, planes, 8, radial), F32)] + [pltpu.VMEM(plane, F32)] * 3,
        compiler_params=params(),
        name="last",
    )(
        axial, ghost, below, came_side, to_third, to_zero, to_lower, second, top,
        right_other, partial, blocks, state,
    )
    return residual, new_state


def solution(mesh):
    return jax.shard_map(
        per_device,
        mesh=mesh,
        in_specs=(
            P("row", None, "slab", "sector", None),
            P("row", None, "slab", "sector", None),
            P("row", None, None, "slab", "sector", None),
            P("row", None, None),
            P("row", None, None, None),
            P(),
        ),
        out_specs=(P("row", None, "slab", "sector", None), P("row", None, "slab", "sector", None)),
        check_vma=False,
    )
```

```python
import jax
import jax.numpy as jnp
from jax import lax
from jax.experimental import pallas as pl
from jax.experimental.pallas import tpu as pltpu
from jax.sharding import PartitionSpec as P

F32 = jnp.float32
V = 5
AXES = ("row", "sector", "slab")
VMEM_BYTES = 14 * 1024 * 1024


def matvec(mat, vec):
    out = []
    for i in range(V):
        acc = mat(i, 0) * vec[0]
        for j in range(1, V):
            acc = acc + mat(i, j) * vec[j]
        out.append(acc)
    return out


def stacked(ref, base):
    return lambda i, j: ref[base + V * i + j]


def planes_of(ref, base):
    return [ref[base + v] for v in range(V)]


def put(ref, base, values):
    for v in range(V):
        ref[base + v] = values[v]


def sliding(owner, columns, total):
    lead = owner[0]

    def lower(i, best):
        return jnp.minimum(best, ((owner[i] - lead + total // 2) & (total - 1)) - total // 2)

    return (lead + lax.fori_loop(1, columns, lower, jnp.int32(0), unroll=True)) & (total - 1)


def pack_kernel(
    planes, columns, state, towards_low, interface, towards_high, lowest,
):
    row = lax.axis_index("row")
    face = jnp.where(row == 0, planes - 1, 0)
    for v in range(V):
        plane = state[0, v, face]
        interface[v] = plane
        towards_low[v, planes:] = plane
        lowest[v] = state[0, v, 0]
        for x in range(planes):
            towards_low[v, x : x + 1] = state[0, v, x, 0:1]
            towards_high[v, x : x + 1] = state[0, v, x, columns - 1 : columns]


def load_kernel(inverse, lowest, blocks, arrived):
    copy = pltpu.make_async_copy(inverse, blocks, arrived)
    copy.start()
    copy.wait()


def halved(ref, which=0):
    entries = [
        [jnp.broadcast_to(0.5 * ref[i, which : which + 1, j : j + 1], (8, 128)) for j in range(V)]
        for i in range(V)
    ]
    return lambda i, j: entries[i][j]


def window_kernel(planes, columns, sectors, owner, own, next_one, next_two, message, pair, table, landing):
    row = lax.axis_index("row")
    sector = lax.axis_index("sector")
    total = sectors * columns
    for v in range(V):
        table[v, 0:columns] = own[v]
        table[v, columns : 2 * columns] = next_one[v, planes:]
        table[v, 2 * columns :] = next_two[v]
    turn = sliding(owner, columns, total) >> (columns.bit_length() - 1)
    even = turn & -2
    pair[0] = turn >> 1

    @pl.when(row == 1)
    def _():
        facing = (sector - even) & (sectors - 1)

        def step(i, carry):
            at = (owner[facing * columns + i] - sector * columns) & (total - 1)
            at = jnp.minimum(at, 3 * columns - 1)
            for v in range(V):
                landing[v, pl.ds(i, 1)] = table[v, pl.ds(at, 1)]
            return carry

        lax.fori_loop(0, columns, step, 0, unroll=8)

    @pl.when(row == 0)
    def _():
        facing = (sector + even + 2) & (sectors - 1)
        first = (1 - (turn - even)) * columns

        def step(i, carry):
            at = first + i
            column = owner[(sector * columns + at) & (total - 1)]
            to = jnp.minimum((column - facing * columns) & (total - 1), columns)
            for v in range(V):
                landing[v, pl.ds(to, 1)] = table[v, pl.ds(at, 1)]
            return carry

        lax.fori_loop(0, 2 * columns, step, 0, unroll=8)

    for v in range(V):
        message[v] = landing[v, 0:columns]


def matrix_kernel(
    planes, axial, inverse, prefix_out, right, left, product, prefix, left_now, right_now,
):
    row = lax.axis_index("row")
    slab = lax.axis_index("slab")
    scaled = halved(axial)

    def one_strip(step, carry):
        at = pl.ds(pl.multiple_of(step * 8, 8), 8)

        def factor(x):
            return lambda i, j: product[x, V * i + j]

        def flux_times(x):
            for i in range(V):
                entries = [inverse[0, i, k, x, at] for k in range(V)]
                for j in range(V):
                    acc = entries[0] * scaled(0, j)
                    for k in range(1, V):
                        acc = acc + entries[k] * scaled(k, j)
                    product[x, V * i + j] = acc

        def forward(x, carry):
            flux_times(x)
            for j in range(V):
                column = [prefix[x - 1, V * i + j] for i in range(V)]
                put_column(prefix.at[x], j, matvec(factor(x), column))
            return carry

        flux_times(0)
        for k in range(V * V):
            prefix[0, k] = product[0, k]
        lax.fori_loop(1, planes, forward, 0)
        for k in range(V * V):
            prefix_out[k, at] = prefix[planes - 1, k]

        @pl.when(slab > 0)
        def _():
            for j in range(V):
                column = [prefix[planes - 2, V * i + j] for i in range(V)]
                put_column(left_now, j, matvec(factor(planes - 1), column))

            def backward(step, carry):
                x = planes - 1 - step
                for j in range(V):
                    column = [prefix[x - 1, V * i + j] - left_now[V * i + j] for i in range(V)]
                    put_column(left_now, j, matvec(factor(x), column))
                return carry

            lax.fori_loop(1, planes - 1, backward, 0)
            for j in range(V):
                column = [float(i == j) - left_now[V * i + j] for i in range(V)]
                put_column(left_now, j, matvec(factor(0), column))
            for k in range(V * V):
                left[k, at] = left_now[k]

        @pl.when((slab == 1) | (slab == 2) | ((slab == 3) & (row == 0)))
        def _():
            for k in range(V * V):
                right_now[k] = product[planes - 1, k]

            def backward(step, carry):
                x = planes - 1 - step
                for j in range(V):
                    column = [right_now[V * i + j] for i in range(V)]
                    put_column(right_now, j, matvec(factor(x), column))
                return carry

            lax.fori_loop(1, planes, backward, 0)
            for k in range(V * V):
                right[k, at] = right_now[k]

        return carry

    lax.fori_loop(0, inverse.shape[4] // 8, one_strip, 0)


def put_column(ref, j, values):
    for i in range(V):
        ref[V * i + j] = values[i]


def residual_kernel(
    planes, columns, axial, cross, state, source, inverse, from_high, from_low, above, prefix_in,
    residual, up, down, wide, forward,
):
    for v in range(V):
        for x in range(planes):
            wide[v, x, 8 : 8 + columns] = state[0, v, x]
            wide[v, x, 7:8] = from_low[v, x : x + 1]
            wide[v, x, 8 + columns : 9 + columns] = from_high[v, x : x + 1]
    rows = lax.broadcasted_iota(jnp.int32, (8, 128), 0)
    lanes = lax.broadcasted_iota(jnp.int32, (8, 128), 1)
    ja = halved(axial)
    jb = halved(cross)
    jr = halved(cross, 1)

    def one_strip(step, carry):
        at = pl.ds(pl.multiple_of(step * 8, 8), 8)
        middle = pl.ds(pl.multiple_of(step * 8 + 8, 8), 8)
        high = pl.ds(pl.multiple_of(step * 8 + 16, 8), 8)
        previous = None
        for x in range(planes):
            along, around, outward = [], [], []
            for v in range(V):
                here = wide[v, x, middle]
                nearer = wide[v, x + 1, middle] if x + 1 < planes else above[v, at]
                along.append(nearer - wide[v, x - 1, middle] if x else nearer)
                plus = jnp.where(rows == 0, wide[v, x, high], here)
                minus = jnp.where(rows == 7, wide[v, x, at], here)
                around.append(pltpu.roll(plus, 7, 0) - pltpu.roll(minus, 1, 0))
                outward.append(
                    jnp.where(lanes == 127, 0.0, pltpu.roll(here, 127, 1))
                    - jnp.where(lanes == 0, 0.0, pltpu.roll(here, 1, 1))
                )
            one, two, three = matvec(ja, along), matvec(jb, around), matvec(jr, outward)
            values = [source[0, v, x, at] - (one[v] + two[v] + three[v]) for v in range(V)]
            for v in range(V):
                residual[v, x, at] = values[v]
            if previous is not None:
                carried = matvec(ja, previous)
                values = [values[v] + carried[v] for v in range(V)]
            previous = matvec(lambda i, j: inverse[0, i, j, x, at], values)
            for v in range(V):
                forward[v, x] = previous[v]
        for v in range(V):
            last = wide[v, planes - 1, middle]
            up[v, at] = previous[v] + last
        for k in range(V * V):
            up[V + k, at] = prefix_in[k, at]
        for v in range(V):
            up[V + V * V + v, at] = wide[v, planes - 1, middle]
        for x in range(planes - 2, -1, -1):
            carried = matvec(lambda i, j: inverse[0, i, j, x, at], matvec(ja, previous))
            previous = [forward[v, x] - carried[v] for v in range(V)]
        for v in range(V):
            down[v, at] = previous[v]
        return carry

    lax.fori_loop(0, columns // 8, one_strip, 0)


def first_kernel(ghost, up, down, right, entry, message):
    slab = lax.axis_index("slab")

    @pl.when(slab == 0)
    def _():
        moved = matvec(stacked(up, V), planes_of(ghost, 0))
        for v in range(V):
            total = up[v] + moved[v]
            entry[v] = total
            message[v] = total

    @pl.when(slab == 3)
    def _():
        moved = matvec(stacked(right, 0), planes_of(ghost, 0))
        for v in range(V):
            message[v] = jnp.where(lax.axis_index("row") == 0, down[v] + moved[v], down[v])


def middle_kernel(came, came_side, up_other, left_other, up, down, right, left, lower, third, second, top):
    slab = lax.axis_index("slab")

    @pl.when(slab == 1)
    def _():
        moved = matvec(stacked(left, 0), planes_of(came_side, 0))
        put(lower, 0, [down[v] + moved[v] for v in range(V)])

    @pl.when(slab == 2)
    def _():
        moved = matvec(stacked(up_other, V), planes_of(came, 0))
        inflow = [up_other[v] + moved[v] for v in range(V)]
        moved = matvec(stacked(up, V), inflow)
        onward = [up[v] + moved[v] for v in range(V)]
        moved = matvec(stacked(left_other, 0), onward)
        beyond = [came_side[v] + moved[v] for v in range(V)]
        moved = matvec(stacked(left, 0), inflow)
        again = matvec(stacked(right, 0), beyond)
        put(lower, 0, [down[v] + moved[v] + again[v] for v in range(V)])
        put(third, 0, onward)
        put(second, 0, inflow)
        put(top, 0, beyond)


def last_kernel(
    planes, axial, ghost, up_other, came_side, to_third, to_zero, to_lower, second, top,
    right_other, partial, inverse, state, residual, new_state, forward, inflow, beyond, under,
):
    row = lax.axis_index("row")
    slab = lax.axis_index("slab")
    ja = halved(axial)
    has_top = jnp.where((row == 0) & (slab == 3), 1.0, 0.0)

    at = pl.ds(pl.multiple_of(pl.program_id(0) * 8, 8), 8)

    def fetch(ref, base=0):
        return [ref[base + v, at] for v in range(V)]

    @pl.when(slab == 0)
    def _():
        put(inflow, 0, fetch(ghost))
        put(under, 0, fetch(ghost))
        moved = matvec(lambda i, j: right_other[V * i + j, at], fetch(to_zero))
        put(beyond, 0, [to_lower[v, at] + moved[v] for v in range(V)])

    @pl.when(slab != 0)
    def _():
        put(under, 0, fetch(up_other, V + V * V))

    @pl.when(slab == 1)
    def _():
        put(inflow, 0, fetch(came_side))
        put(beyond, 0, fetch(to_lower))

    @pl.when(slab == 2)
    def _():
        put(inflow, 0, fetch(second))
        put(beyond, 0, fetch(top))

    @pl.when(slab == 3)
    def _():
        put(inflow, 0, fetch(to_third))
        put(beyond, 0, [jnp.zeros((8, 128), F32)] * V)

    previous = planes_of(inflow, 0)
    for x in range(planes):
        values = [partial[v, x, at] for v in range(V)]
        if x == planes - 1:
            top_part = matvec(ja, [ghost[v, at] * has_top for v in range(V)])
            values = [values[v] - top_part[v] for v in range(V)]
        if x == 0:
            bottom = matvec(ja, planes_of(under, 0))
            for v in range(V):
                residual[0, v, x] = values[v] + bottom[v]
        else:
            for v in range(V):
                residual[0, v, x] = values[v]
        carried = matvec(ja, previous)
        values = [values[v] + carried[v] for v in range(V)]
        previous = matvec(lambda i, j: inverse[0, i, j, x, at], values)
        for v in range(V):
            forward[v, x] = previous[v]
    following = planes_of(beyond, 0)
    for x in range(planes - 1, -1, -1):
        carried = matvec(lambda i, j: inverse[0, i, j, x, at], matvec(ja, following))
        following = [forward[v, x] - carried[v] for v in range(V)]
        for v in range(V):
            new_state[0, v, x] = state[0, v, x, at] + following[v]


def near(*shape):
    return pltpu.VMEM(shape, F32)


def sds(*shape):
    return jax.ShapeDtypeStruct(shape, F32)


SCALARS = pl.BlockSpec(memory_space=pltpu.SMEM)
WHOLE = pl.BlockSpec(memory_space=pltpu.VMEM)


def params(**more):
    return pltpu.CompilerParams(vmem_limit_bytes=VMEM_BYTES, **more)


def cost(amount):
    return pl.CostEstimate(flops=amount, bytes_accessed=amount // 8, transcendentals=0)


def per_device(state, source, diag_inverse, jac_axial, jac_cross, owner):
    planes, columns, radial = state.shape[2:]
    sectors = lax.axis_size("sector")
    slabs = lax.axis_size("slab")
    plane = (V, columns, radial)
    cells = pl.BlockSpec((1, V, planes, 8, radial), lambda i: (0, 0, 0, i, 0))
    size = slabs * sectors

    def device(row, sector, slab):
        return row * size + sector % sectors * slabs + slab

    def import_pairs(even):
        pairs = []
        for j in range(sectors):
            pairs.append((device(1, j, 0), device(0, j - even, slabs - 1)))
            pairs.append((device(0, j, slabs - 1), device(1, j + even + 2, 0)))
        return pairs

    two_down = []
    for j in range(sectors):
        two_down.append((device(0, j, slabs - 1), device(0, j - 2, slabs - 1)))
        two_down.append((device(1, j, 0), device(1, j - 2, 0)))

    total = sectors * columns
    assert total & (total - 1) == 0 and columns & (columns - 1) == 0
    axial = jnp.transpose(jac_axial, (1, 0, 2))
    cross = jnp.transpose(jac_cross[0], (1, 0, 2))
    towards_low, interface, towards_high, lowest = pl.pallas_call(
        lambda *refs: pack_kernel(planes, columns, *refs),
        out_shape=(near(V, planes + columns, radial), near(*plane), near(V, planes, radial), near(*plane)),
        compiler_params=params(),
        name="pack",
    )(state)
    above = lax.ppermute(lowest, "slab", [(k, k - 1) for k in range(1, slabs)])
    from_low = lax.ppermute(towards_high, "sector", [(j, (j + 1) % sectors) for j in range(sectors)])
    from_second = lax.ppermute(interface, AXES, two_down)
    from_high = lax.ppermute(towards_low, "sector", [(j, (j - 1) % sectors) for j in range(sectors)])

    square = near(V * V, columns, radial)
    blocks = pl.pallas_call(
        load_kernel,
        in_specs=[pl.BlockSpec(memory_space=pltpu.HBM), pl.BlockSpec(memory_space=pl.ANY)],
        out_specs=WHOLE,
        out_shape=near(*diag_inverse.shape),
        scratch_shapes=[pltpu.SemaphoreType.DMA],
        compiler_params=params(),
        cost_estimate=cost(20_000_000),
        name="load",
    )(pltpu.with_memory_space_constraint(diag_inverse, pltpu.HBM), lowest)
    message, pair = pl.pallas_call(
        lambda *refs: window_kernel(planes, columns, sectors, *refs),
        in_specs=[SCALARS] + [WHOLE] * 3,
        out_specs=[WHOLE, SCALARS],
        out_shape=(near(*plane), jax.ShapeDtypeStruct((1,), jnp.int32)),
        scratch_shapes=[
            pltpu.VMEM((V, 3 * columns, radial), F32),
            pltpu.VMEM((V, columns + 8, radial), F32),
        ],
        compiler_params=params(),
        name="window",
    )(owner, interface, from_high, from_second)

    def exchange(even, message, from_low, above, from_high, blocks):
        ghost = lax.ppermute(message, AXES, import_pairs(even))
        prefix, right, left = pl.pallas_call(
            lambda *refs: matrix_kernel(planes, *refs),
            in_specs=[WHOLE, WHOLE],
            out_shape=(square, square, square),
            scratch_shapes=[
                pltpu.VMEM((planes, V * V, 8, radial), F32),
                pltpu.VMEM((planes, V * V, 8, radial), F32),
                pltpu.VMEM((V * V, 8, radial), F32),
                pltpu.VMEM((V * V, 8, radial), F32),
            ],
            compiler_params=params(),
            cost_estimate=cost(60_000_000),
            name="matrices",
        )(axial, blocks)
        partial, up, down = pl.pallas_call(
            lambda *refs: residual_kernel(planes, columns, *refs),
            in_specs=[WHOLE] * 9,
            out_shape=(
                near(V, planes, columns, radial), near(2 * V + V * V, columns, radial), near(*plane),
            ),
            scratch_shapes=[
                pltpu.VMEM((V, planes, columns + 16, radial), F32),
                pltpu.VMEM((V, planes, 8, radial), F32),
            ],
            compiler_params=params(),
            cost_estimate=cost(40_000_000),
            name="residual",
        )(axial, cross, state, source, blocks, from_high, from_low, above, prefix)
        return ghost, partial, up, down, right, left

    ghost, partial, up, down, right, left = lax.switch(
        pair[0],
        [lambda *args, e=e: exchange(2 * e, *args) for e in range(sectors // 2)],
        message, from_low, above, from_high, blocks,
    )
    up_other = lax.ppermute(up, "slab", [(k, k + 1) for k in range(slabs - 1)])
    left_other = lax.ppermute(left, "slab", [(3, 2)])
    entry, side_message = pl.pallas_call(
        first_kernel,
        out_shape=(near(*plane), near(*plane)),
        compiler_params=params(),
        name="first",
    )(ghost, up, down, right)
    came_side = lax.ppermute(side_message, "slab", [(0, 1), (3, 2)])
    came = lax.ppermute(entry, "slab", [(0, 2)])
    right, came, came_side = lax.optimization_barrier((right, came, came_side))
    right_other = lax.ppermute(right, "slab", [(1, 0)])
    lower, onward, second, top = pl.pallas_call(
        middle_kernel,
        out_shape=(near(*plane),) * 4,
        compiler_params=params(),
        name="middle",
    )(came, came_side, up_other, left_other, up, down, right, left)
    to_lower = lax.ppermute(lower, "slab", [(2, 1), (1, 0)])
    to_third = lax.ppermute(onward, "slab", [(2, 3)])
    to_zero = lax.ppermute(lower, "slab", [(2, 0)])

    residual, new_state = pl.pallas_call(
        lambda *refs: last_kernel(planes, *refs),
        grid=(columns // 8,),
        in_specs=[WHOLE] * 13,
        out_specs=(cells, cells),
        out_shape=(sds(*state.shape), sds(*state.shape)),
        scratch_shapes=[pltpu.VMEM((V, planes, 8, radial), F32)] + [pltpu.VMEM((V, 8, radial), F32)] * 3,
        compiler_params=params(),
        name="last",
    )(
        axial, ghost, up_other, came_side, to_third, to_zero, to_lower, second, top,
        right_other, partial, blocks, state,
    )
    return residual, new_state


def solution(mesh):
    return jax.shard_map(
        per_device,
        mesh=mesh,
        in_specs=(
            P("row", None, "slab", "sector", None),
            P("row", None, "slab", "sector", None),
            P("row", None, None, "slab", "sector", None),
            P("row", None, None),
            P("row", None, None, None),
            P(),
        ),
        out_specs=(P("row", None, "slab", "sector", None), P("row", None, "slab", "sector", None)),
        check_vma=False,
    )
```

```python
import jax
import jax.numpy as jnp
from jax import lax
from jax.experimental import pallas as pl
from jax.experimental.pallas import tpu as pltpu
from jax.sharding import PartitionSpec as P

F32 = jnp.float32
V = 5
AXES = ("row", "sector", "slab")
VMEM_BYTES = 14 * 1024 * 1024


def matvec(mat, vec):
    out = []
    for i in range(V):
        acc = mat(i, 0) * vec[0]
        for j in range(1, V):
            acc = acc + mat(i, j) * vec[j]
        out.append(acc)
    return out


def stacked(ref, base):
    return lambda i, j: ref[base + V * i + j]


def planes_of(ref, base):
    return [ref[base + v] for v in range(V)]


def put(ref, base, values):
    for v in range(V):
        ref[base + v] = values[v]


def sliding(owner, columns, total):
    lead = owner[0]

    def lower(i, best):
        return jnp.minimum(best, ((owner[i] - lead + total // 2) & (total - 1)) - total // 2)

    return (lead + lax.fori_loop(1, columns, lower, jnp.int32(0), unroll=True)) & (total - 1)


def pack_kernel(
    planes, columns, state, towards_low, interface, towards_high, lowest,
):
    row = lax.axis_index("row")
    face = jnp.where(row == 0, planes - 1, 0)
    for v in range(V):
        plane = state[0, v, face]
        interface[v] = plane
        towards_low[v, planes:] = plane
        lowest[v] = state[0, v, 0]
        for x in range(planes):
            towards_low[v, x : x + 1] = state[0, v, x, 0:1]
            towards_high[v, x : x + 1] = state[0, v, x, columns - 1 : columns]


def load_kernel(inverse, lowest, blocks, arrived):
    copy = pltpu.make_async_copy(inverse, blocks, arrived)
    copy.start()
    copy.wait()


def halved(ref, which=0):
    entries = [
        [jnp.broadcast_to(0.5 * ref[i, which : which + 1, j : j + 1], (8, 128)) for j in range(V)]
        for i in range(V)
    ]
    return lambda i, j: entries[i][j]


def window_kernel(planes, columns, sectors, owner, own, next_one, next_two, message, pair, table, landing):
    row = lax.axis_index("row")
    sector = lax.axis_index("sector")
    total = sectors * columns
    for v in range(V):
        table[v, 0:columns] = own[v]
        table[v, columns : 2 * columns] = next_one[v, planes:]
        table[v, 2 * columns :] = next_two[v]
    turn = sliding(owner, columns, total) >> (columns.bit_length() - 1)
    even = turn & -2
    pair[0] = turn >> 1

    @pl.when(row == 1)
    def _():
        facing = (sector - even) & (sectors - 1)

        def step(i, carry):
            at = (owner[facing * columns + i] - sector * columns) & (total - 1)
            at = jnp.minimum(at, 3 * columns - 1)
            for v in range(V):
                landing[v, pl.ds(i, 1)] = table[v, pl.ds(at, 1)]
            return carry

        lax.fori_loop(0, columns, step, 0, unroll=8)

    @pl.when(row == 0)
    def _():
        facing = (sector + even + 2) & (sectors - 1)
        first = (1 - (turn - even)) * columns

        def step(i, carry):
            at = first + i
            column = owner[(sector * columns + at) & (total - 1)]
            to = jnp.minimum((column - facing * columns) & (total - 1), columns)
            for v in range(V):
                landing[v, pl.ds(to, 1)] = table[v, pl.ds(at, 1)]
            return carry

        lax.fori_loop(0, 2 * columns, step, 0, unroll=8)

    for v in range(V):
        message[v] = landing[v, 0:columns]


def matrix_kernel(
    planes, axial, inverse, prefix_out, right, left, side, product, prefix, left_now, right_now,
):
    row = lax.axis_index("row")
    slab = lax.axis_index("slab")
    scaled = halved(axial)

    def one_strip(step, carry):
        at = pl.ds(pl.multiple_of(step * 8, 8), 8)

        def factor(x):
            return lambda i, j: product[x, V * i + j]

        def flux_times(x):
            for i in range(V):
                entries = [inverse[0, i, k, x, at] for k in range(V)]
                for j in range(V):
                    acc = entries[0] * scaled(0, j)
                    for k in range(1, V):
                        acc = acc + entries[k] * scaled(k, j)
                    product[x, V * i + j] = acc

        def forward(x, carry):
            flux_times(x)
            for j in range(V):
                column = [prefix[x - 1, V * i + j] for i in range(V)]
                put_column(prefix.at[x], j, matvec(factor(x), column))
            return carry

        flux_times(0)
        for k in range(V * V):
            prefix[0, k] = product[0, k]
        lax.fori_loop(1, planes, forward, 0)
        for k in range(V * V):
            prefix_out[k, at] = prefix[planes - 1, k]

        @pl.when(slab > 0)
        def _():
            for j in range(V):
                column = [prefix[planes - 2, V * i + j] for i in range(V)]
                put_column(left_now, j, matvec(factor(planes - 1), column))

            def backward(step, carry):
                x = planes - 1 - step
                for j in range(V):
                    column = [prefix[x - 1, V * i + j] - left_now[V * i + j] for i in range(V)]
                    put_column(left_now, j, matvec(factor(x), column))
                return carry

            lax.fori_loop(1, planes - 1, backward, 0)
            for j in range(V):
                column = [float(i == j) - left_now[V * i + j] for i in range(V)]
                put_column(left_now, j, matvec(factor(0), column))
            for k in range(V * V):
                left[k, at] = left_now[k]
                side[k, at] = left_now[k]

        @pl.when((slab == 1) | (slab == 2) | ((slab == 3) & (row == 0)))
        def _():
            for k in range(V * V):
                right_now[k] = product[planes - 1, k]

            def backward(step, carry):
                x = planes - 1 - step
                for j in range(V):
                    column = [right_now[V * i + j] for i in range(V)]
                    put_column(right_now, j, matvec(factor(x), column))
                return carry

            lax.fori_loop(1, planes, backward, 0)
            for k in range(V * V):
                right[k, at] = right_now[k]

        @pl.when(slab == 1)
        def _():
            for k in range(V * V):
                side[k, at] = right_now[k]


        return carry

    lax.fori_loop(0, inverse.shape[4] // 8, one_strip, 0)


def put_column(ref, j, values):
    for i in range(V):
        ref[V * i + j] = values[i]


def residual_kernel(
    planes, columns, axial, cross, state, source, inverse, from_high, from_low, above, prefix_in,
    residual, up, down, wide, forward,
):
    for v in range(V):
        for x in range(planes):
            wide[v, x, 8 : 8 + columns] = state[0, v, x]
            wide[v, x, 7:8] = from_low[v, x : x + 1]
            wide[v, x, 8 + columns : 9 + columns] = from_high[v, x : x + 1]
    rows = lax.broadcasted_iota(jnp.int32, (8, 128), 0)
    lanes = lax.broadcasted_iota(jnp.int32, (8, 128), 1)
    ja = halved(axial)
    jb = halved(cross)
    jr = halved(cross, 1)

    def one_strip(step, carry):
        at = pl.ds(pl.multiple_of(step * 8, 8), 8)
        middle = pl.ds(pl.multiple_of(step * 8 + 8, 8), 8)
        high = pl.ds(pl.multiple_of(step * 8 + 16, 8), 8)
        previous = None
        for x in range(planes):
            along, around, outward = [], [], []
            for v in range(V):
                here = wide[v, x, middle]
                nearer = wide[v, x + 1, middle] if x + 1 < planes else above[v, at]
                along.append(nearer - wide[v, x - 1, middle] if x else nearer)
                plus = jnp.where(rows == 0, wide[v, x, high], here)
                minus = jnp.where(rows == 7, wide[v, x, at], here)
                around.append(pltpu.roll(plus, 7, 0) - pltpu.roll(minus, 1, 0))
                outward.append(
                    jnp.where(lanes == 127, 0.0, pltpu.roll(here, 127, 1))
                    - jnp.where(lanes == 0, 0.0, pltpu.roll(here, 1, 1))
                )
            one, two, three = matvec(ja, along), matvec(jb, around), matvec(jr, outward)
            values = [source[0, v, x, at] - (one[v] + two[v] + three[v]) for v in range(V)]
            for v in range(V):
                residual[v, x, at] = values[v]
            if previous is not None:
                carried = matvec(ja, previous)
                values = [values[v] + carried[v] for v in range(V)]
            previous = matvec(lambda i, j: inverse[0, i, j, x, at], values)
            for v in range(V):
                forward[v, x] = previous[v]
        for v in range(V):
            last = wide[v, planes - 1, middle]
            up[v, at] = previous[v] + last
        for k in range(V * V):
            up[V + k, at] = prefix_in[k, at]
        for v in range(V):
            up[V + V * V + v, at] = wide[v, planes - 1, middle]
        for x in range(planes - 2, -1, -1):
            carried = matvec(lambda i, j: inverse[0, i, j, x, at], matvec(ja, previous))
            previous = [forward[v, x] - carried[v] for v in range(V)]
        for v in range(V):
            down[v, at] = previous[v]
        return carry

    lax.fori_loop(0, columns // 8, one_strip, 0)


def first_kernel(ghost, up, down, right, side, entry, packed):
    slab = lax.axis_index("slab")

    @pl.when((slab == 1) | (slab == 3))
    def _():
        packed[V:] = side[...]

    @pl.when(slab == 0)
    def _():
        moved = matvec(stacked(up, V), planes_of(ghost, 0))
        put(entry, 0, [up[v] + moved[v] for v in range(V)])

    @pl.when(slab == 3)
    def _():
        moved = matvec(stacked(right, 0), planes_of(ghost, 0))
        for v in range(V):
            packed[v] = jnp.where(lax.axis_index("row") == 0, down[v] + moved[v], down[v])


def middle_kernel(came, came_side, up_other, side_other, up, down, right, left, lower, third, second, top):
    slab = lax.axis_index("slab")

    put(third, V, planes_of(up, V + V * V))

    @pl.when(slab == 1)
    def _():
        moved = matvec(stacked(left, 0), planes_of(came_side, 0))
        put(lower, 0, [down[v] + moved[v] for v in range(V)])

    @pl.when(slab == 2)
    def _():
        moved = matvec(stacked(up_other, V), planes_of(came, 0))
        inflow = [up_other[v] + moved[v] for v in range(V)]
        moved = matvec(stacked(up, V), inflow)
        onward = [up[v] + moved[v] for v in range(V)]
        moved = matvec(stacked(side_other, V), onward)
        beyond = [side_other[v] + moved[v] for v in range(V)]
        moved = matvec(stacked(left, 0), inflow)
        again = matvec(stacked(right, 0), beyond)
        put(lower, 0, [down[v] + moved[v] + again[v] for v in range(V)])
        put(third, 0, onward)
        put(second, 0, inflow)
        put(top, 0, beyond)


def last_kernel(
    planes, axial, ghost, up_other, came_side, to_third, to_zero, to_lower, second, top,
    side_other, partial, inverse, state, residual, new_state, forward, inflow, beyond, under,
):
    row = lax.axis_index("row")
    slab = lax.axis_index("slab")
    ja = halved(axial)
    has_top = jnp.where((row == 0) & (slab == 3), 1.0, 0.0)

    at = pl.ds(pl.multiple_of(pl.program_id(0) * 8, 8), 8)

    def fetch(ref, base=0):
        return [ref[base + v, at] for v in range(V)]

    @pl.when(slab == 0)
    def _():
        put(inflow, 0, fetch(ghost))
        put(under, 0, fetch(ghost))
        moved = matvec(lambda i, j: side_other[V + V * i + j, at], fetch(to_zero))
        put(beyond, 0, [to_lower[v, at] + moved[v] for v in range(V)])

    @pl.when(slab == 1)
    def _():
        put(inflow, 0, fetch(came_side))
        put(under, 0, fetch(to_third, V))
        put(beyond, 0, fetch(to_lower))

    @pl.when(slab == 2)
    def _():
        put(inflow, 0, fetch(second))
        put(under, 0, fetch(up_other, V + V * V))
        put(beyond, 0, fetch(top))

    @pl.when(slab == 3)
    def _():
        put(inflow, 0, fetch(to_third))
        put(under, 0, fetch(to_third, V))
        put(beyond, 0, [jnp.zeros((8, 128), F32)] * V)

    previous = planes_of(inflow, 0)
    for x in range(planes):
        values = [partial[v, x, at] for v in range(V)]
        if x == planes - 1:
            top_part = matvec(ja, [ghost[v, at] * has_top for v in range(V)])
            values = [values[v] - top_part[v] for v in range(V)]
        if x == 0:
            bottom = matvec(ja, planes_of(under, 0))
            for v in range(V):
                residual[0, v, x] = values[v] + bottom[v]
        else:
            for v in range(V):
                residual[0, v, x] = values[v]
        carried = matvec(ja, previous)
        values = [values[v] + carried[v] for v in range(V)]
        previous = matvec(lambda i, j: inverse[0, i, j, x, at], values)
        for v in range(V):
            forward[v, x] = previous[v]
    following = planes_of(beyond, 0)
    for x in range(planes - 1, -1, -1):
        carried = matvec(lambda i, j: inverse[0, i, j, x, at], matvec(ja, following))
        following = [forward[v, x] - carried[v] for v in range(V)]
        for v in range(V):
            new_state[0, v, x] = state[0, v, x, at] + following[v]


def near(*shape):
    return pltpu.VMEM(shape, F32)


def sds(*shape):
    return jax.ShapeDtypeStruct(shape, F32)


SCALARS = pl.BlockSpec(memory_space=pltpu.SMEM)
WHOLE = pl.BlockSpec(memory_space=pltpu.VMEM)


def params(**more):
    return pltpu.CompilerParams(vmem_limit_bytes=VMEM_BYTES, **more)


def cost(amount):
    return pl.CostEstimate(flops=amount, bytes_accessed=amount // 8, transcendentals=0)


def per_device(state, source, diag_inverse, jac_axial, jac_cross, owner):
    planes, columns, radial = state.shape[2:]
    sectors = lax.axis_size("sector")
    slabs = lax.axis_size("slab")
    plane = (V, columns, radial)
    cells = pl.BlockSpec((1, V, planes, 8, radial), lambda i: (0, 0, 0, i, 0))
    size = slabs * sectors

    def device(row, sector, slab):
        return row * size + sector % sectors * slabs + slab

    def import_pairs(even):
        pairs = []
        for j in range(sectors):
            pairs.append((device(1, j, 0), device(0, j - even, slabs - 1)))
            pairs.append((device(0, j, slabs - 1), device(1, j + even + 2, 0)))
        return pairs

    two_down = []
    for j in range(sectors):
        two_down.append((device(0, j, slabs - 1), device(0, j - 2, slabs - 1)))
        two_down.append((device(1, j, 0), device(1, j - 2, 0)))

    total = sectors * columns
    assert total & (total - 1) == 0 and columns & (columns - 1) == 0
    axial = jnp.transpose(jac_axial, (1, 0, 2))
    cross = jnp.transpose(jac_cross[0], (1, 0, 2))
    towards_low, interface, towards_high, lowest = pl.pallas_call(
        lambda *refs: pack_kernel(planes, columns, *refs),
        out_shape=(near(V, planes + columns, radial), near(*plane), near(V, planes, radial), near(*plane)),
        compiler_params=params(),
        name="pack",
    )(state)
    above = lax.ppermute(lowest, "slab", [(k, k - 1) for k in range(1, slabs)])
    from_low = lax.ppermute(towards_high, "sector", [(j, (j + 1) % sectors) for j in range(sectors)])
    from_second = lax.ppermute(interface, AXES, two_down)
    from_high = lax.ppermute(towards_low, "sector", [(j, (j - 1) % sectors) for j in range(sectors)])

    square = near(V * V, columns, radial)
    blocks = pl.pallas_call(
        load_kernel,
        in_specs=[pl.BlockSpec(memory_space=pltpu.HBM), pl.BlockSpec(memory_space=pl.ANY)],
        out_specs=WHOLE,
        out_shape=near(*diag_inverse.shape),
        scratch_shapes=[pltpu.SemaphoreType.DMA],
        compiler_params=params(),
        cost_estimate=cost(20_000_000),
        name="load",
    )(pltpu.with_memory_space_constraint(diag_inverse, pltpu.HBM), lowest)
    message, pair = pl.pallas_call(
        lambda *refs: window_kernel(planes, columns, sectors, *refs),
        in_specs=[SCALARS] + [WHOLE] * 3,
        out_specs=[WHOLE, SCALARS],
        out_shape=(near(*plane), jax.ShapeDtypeStruct((1,), jnp.int32)),
        scratch_shapes=[
            pltpu.VMEM((V, 3 * columns, radial), F32),
            pltpu.VMEM((V, columns + 8, radial), F32),
        ],
        compiler_params=params(),
        name="window",
    )(owner, interface, from_high, from_second)

    def exchange(even, message, from_low, above, from_high, blocks):
        ghost = lax.ppermute(message, AXES, import_pairs(even))
        prefix, right, left, side = pl.pallas_call(
            lambda *refs: matrix_kernel(planes, *refs),
            in_specs=[WHOLE, WHOLE],
            out_shape=(square, square, square, square),
            scratch_shapes=[
                pltpu.VMEM((planes, V * V, 8, radial), F32),
                pltpu.VMEM((planes, V * V, 8, radial), F32),
                pltpu.VMEM((V * V, 8, radial), F32),
                pltpu.VMEM((V * V, 8, radial), F32),
            ],
            compiler_params=params(),
            cost_estimate=cost(60_000_000),
            name="matrices",
        )(axial, blocks)
        partial, up, down = pl.pallas_call(
            lambda *refs: residual_kernel(planes, columns, *refs),
            in_specs=[WHOLE] * 9,
            out_shape=(
                near(V, planes, columns, radial), near(2 * V + V * V, columns, radial), near(*plane),
            ),
            scratch_shapes=[
                pltpu.VMEM((V, planes, columns + 16, radial), F32),
                pltpu.VMEM((V, planes, 8, radial), F32),
            ],
            compiler_params=params(),
            cost_estimate=cost(40_000_000),
            name="residual",
        )(axial, cross, state, source, blocks, from_high, from_low, above, prefix)
        return ghost, partial, up, down, right, left, side

    ghost, partial, up, down, right, left, side = lax.switch(
        pair[0],
        [lambda *args, e=e: exchange(2 * e, *args) for e in range(sectors // 2)],
        message, from_low, above, from_high, blocks,
    )
    up_other = lax.ppermute(up, "slab", [(1, 2)])
    entry, packed = pl.pallas_call(
        first_kernel,
        out_shape=(near(*plane), near(V + V * V, columns, radial)),
        compiler_params=params(),
        name="first",
    )(ghost, up, down, right, side)
    side_other = lax.ppermute(packed, "slab", [(1, 0), (3, 2)])
    came = lax.ppermute(entry, "slab", [(0, 2)])
    entry, came = lax.optimization_barrier((entry, came))
    came_side = lax.ppermute(entry, "slab", [(0, 1)])
    lower, onward, second, top = pl.pallas_call(
        middle_kernel,
        out_shape=(near(*plane), near(2 * V, columns, radial), near(*plane), near(*plane)),
        compiler_params=params(),
        name="middle",
    )(came, came_side, up_other, side_other, up, down, right, left)
    to_lower = lax.ppermute(lower, "slab", [(2, 1), (1, 0)])
    to_third = lax.ppermute(onward, "slab", [(2, 3), (0, 1)])
    to_zero = lax.ppermute(lower, "slab", [(2, 0)])

    residual, new_state = pl.pallas_call(
        lambda *refs: last_kernel(planes, *refs),
        grid=(columns // 8,),
        in_specs=[WHOLE] * 13,
        out_specs=(cells, cells),
        out_shape=(sds(*state.shape), sds(*state.shape)),
        scratch_shapes=[pltpu.VMEM((V, planes, 8, radial), F32)] + [pltpu.VMEM((V, 8, radial), F32)] * 3,
        compiler_params=params(),
        name="last",
    )(
        axial, ghost, up_other, came_side, to_third, to_zero, to_lower, second, top,
        side_other, partial, blocks, state,
    )
    return residual, new_state


def solution(mesh):
    return jax.shard_map(
        per_device,
        mesh=mesh,
        in_specs=(
            P("row", None, "slab", "sector", None),
            P("row", None, "slab", "sector", None),
            P("row", None, None, "slab", "sector", None),
            P("row", None, None),
            P("row", None, None, None),
            P(),
        ),
        out_specs=(P("row", None, "slab", "sector", None), P("row", None, "slab", "sector", None)),
        check_vma=False,
    )
```

```python
import jax
import jax.numpy as jnp
from jax import lax
from jax.experimental import pallas as pl
from jax.experimental.pallas import tpu as pltpu
from jax.sharding import PartitionSpec as P

F32 = jnp.float32
V = 5
AXES = ("row", "sector", "slab")
VMEM_BYTES = 14 * 1024 * 1024


def matvec(mat, vec):
    out = []
    for i in range(V):
        acc = mat(i, 0) * vec[0]
        for j in range(1, V):
            acc = acc + mat(i, j) * vec[j]
        out.append(acc)
    return out


def stacked(ref, base):
    return lambda i, j: ref[base + V * i + j]


def planes_of(ref, base):
    return [ref[base + v] for v in range(V)]


def put(ref, base, values):
    for v in range(V):
        ref[base + v] = values[v]


def sliding(owner, columns, total):
    lead = owner[0]

    def lower(i, best):
        return jnp.minimum(best, ((owner[i] - lead + total // 2) & (total - 1)) - total // 2)

    return (lead + lax.fori_loop(1, columns, lower, jnp.int32(0), unroll=True)) & (total - 1)


def pack_kernel(
    planes, columns, state, towards_low, interface, towards_high, lowest,
):
    row = lax.axis_index("row")
    face = jnp.where(row == 0, planes - 1, 0)
    for v in range(V):
        plane = state[0, v, face]
        interface[v] = plane
        towards_low[v, planes:] = plane
        lowest[v] = state[0, v, 0]
        for x in range(planes):
            towards_low[v, x : x + 1] = state[0, v, x, 0:1]
            towards_high[v, x : x + 1] = state[0, v, x, columns - 1 : columns]


def load_kernel(inverse, lowest, blocks, arrived):
    copy = pltpu.make_async_copy(inverse, blocks, arrived)
    copy.start()
    copy.wait()


def halved(ref, which=0):
    entries = [
        [jnp.broadcast_to(0.5 * ref[i, which : which + 1, j : j + 1], (8, 128)) for j in range(V)]
        for i in range(V)
    ]
    return lambda i, j: entries[i][j]


def window_kernel(planes, columns, sectors, owner, own, next_one, next_two, message, pair, table, landing):
    row = lax.axis_index("row")
    sector = lax.axis_index("sector")
    total = sectors * columns
    for v in range(V):
        table[v, 0:columns] = own[v]
        table[v, columns : 2 * columns] = next_one[v, planes:]
        table[v, 2 * columns :] = next_two[v]
    turn = sliding(owner, columns, total) >> (columns.bit_length() - 1)
    even = turn & -2
    pair[0] = turn >> 1

    @pl.when(row == 1)
    def _():
        facing = (sector - even) & (sectors - 1)

        def step(i, carry):
            at = (owner[facing * columns + i] - sector * columns) & (total - 1)
            at = jnp.minimum(at, 3 * columns - 1)
            for v in range(V):
                landing[v, pl.ds(i, 1)] = table[v, pl.ds(at, 1)]
            return carry

        lax.fori_loop(0, columns, step, 0, unroll=8)

    @pl.when(row == 0)
    def _():
        facing = (sector + even + 2) & (sectors - 1)
        first = (1 - (turn - even)) * columns

        def step(i, carry):
            at = first + i
            column = owner[(sector * columns + at) & (total - 1)]
            to = jnp.minimum((column - facing * columns) & (total - 1), columns)
            for v in range(V):
                landing[v, pl.ds(to, 1)] = table[v, pl.ds(at, 1)]
            return carry

        lax.fori_loop(0, 2 * columns, step, 0, unroll=8)

    for v in range(V):
        message[v] = landing[v, 0:columns]


def matrix_kernel(
    planes, axial, inverse, prefix_out, right, left, product, prefix, left_now, right_now,
):
    row = lax.axis_index("row")
    slab = lax.axis_index("slab")
    scaled = halved(axial)

    def one_strip(step, carry):
        at = pl.ds(pl.multiple_of(step * 8, 8), 8)

        def factor(x):
            return lambda i, j: product[x, V * i + j]

        def flux_times(x):
            for i in range(V):
                entries = [inverse[0, i, k, x, at] for k in range(V)]
                for j in range(V):
                    acc = entries[0] * scaled(0, j)
                    for k in range(1, V):
                        acc = acc + entries[k] * scaled(k, j)
                    product[x, V * i + j] = acc

        def forward(x, carry):
            flux_times(x)
            for j in range(V):
                column = [prefix[x - 1, V * i + j] for i in range(V)]
                put_column(prefix.at[x], j, matvec(factor(x), column))
            return carry

        flux_times(0)
        for k in range(V * V):
            prefix[0, k] = product[0, k]
        lax.fori_loop(1, planes, forward, 0)
        for k in range(V * V):
            prefix_out[k, at] = prefix[planes - 1, k]

        @pl.when(slab > 0)
        def _():
            for j in range(V):
                column = [prefix[planes - 2, V * i + j] for i in range(V)]
                put_column(left_now, j, matvec(factor(planes - 1), column))

            def backward(step, carry):
                x = planes - 1 - step
                for j in range(V):
                    column = [prefix[x - 1, V * i + j] - left_now[V * i + j] for i in range(V)]
                    put_column(left_now, j, matvec(factor(x), column))
                return carry

            lax.fori_loop(1, planes - 1, backward, 0)
            for j in range(V):
                column = [float(i == j) - left_now[V * i + j] for i in range(V)]
                put_column(left_now, j, matvec(factor(0), column))
            for k in range(V * V):
                left[k, at] = left_now[k]

        @pl.when((slab == 1) | (slab == 2) | ((slab == 3) & (row == 0)))
        def _():
            for k in range(V * V):
                right_now[k] = product[planes - 1, k]

            def backward(step, carry):
                x = planes - 1 - step
                for j in range(V):
                    column = [right_now[V * i + j] for i in range(V)]
                    put_column(right_now, j, matvec(factor(x), column))
                return carry

            lax.fori_loop(1, planes, backward, 0)
            for k in range(V * V):
                right[k, at] = right_now[k]

        return carry

    lax.fori_loop(0, inverse.shape[4] // 8, one_strip, 0)


def put_column(ref, j, values):
    for i in range(V):
        ref[V * i + j] = values[i]


def residual_kernel(
    planes, columns, axial, cross, state, source, inverse, from_high, from_low, above, prefix_in,
    residual, up, down, wide, forward,
):
    for v in range(V):
        for x in range(planes):
            wide[v, x, 8 : 8 + columns] = state[0, v, x]
            wide[v, x, 7:8] = from_low[v, x : x + 1]
            wide[v, x, 8 + columns : 9 + columns] = from_high[v, x : x + 1]
    rows = lax.broadcasted_iota(jnp.int32, (8, 128), 0)
    lanes = lax.broadcasted_iota(jnp.int32, (8, 128), 1)
    ja = halved(axial)
    jb = halved(cross)
    jr = halved(cross, 1)

    def one_strip(step, carry):
        at = pl.ds(pl.multiple_of(step * 8, 8), 8)
        middle = pl.ds(pl.multiple_of(step * 8 + 8, 8), 8)
        high = pl.ds(pl.multiple_of(step * 8 + 16, 8), 8)
        previous = None
        for x in range(planes):
            along, around, outward = [], [], []
            for v in range(V):
                here = wide[v, x, middle]
                nearer = wide[v, x + 1, middle] if x + 1 < planes else above[v, at]
                along.append(nearer - wide[v, x - 1, middle] if x else nearer)
                plus = jnp.where(rows == 0, wide[v, x, high], here)
                minus = jnp.where(rows == 7, wide[v, x, at], here)
                around.append(pltpu.roll(plus, 7, 0) - pltpu.roll(minus, 1, 0))
                outward.append(
                    jnp.where(lanes == 127, 0.0, pltpu.roll(here, 127, 1))
                    - jnp.where(lanes == 0, 0.0, pltpu.roll(here, 1, 1))
                )
            one, two, three = matvec(ja, along), matvec(jb, around), matvec(jr, outward)
            values = [source[0, v, x, at] - (one[v] + two[v] + three[v]) for v in range(V)]
            for v in range(V):
                residual[v, x, at] = values[v]
            if previous is not None:
                carried = matvec(ja, previous)
                values = [values[v] + carried[v] for v in range(V)]
            previous = matvec(lambda i, j: inverse[0, i, j, x, at], values)
            for v in range(V):
                forward[v, x] = previous[v]
        for v in range(V):
            last = wide[v, planes - 1, middle]
            up[v, at] = previous[v] + last
        for k in range(V * V):
            up[V + k, at] = prefix_in[k, at]
        for v in range(V):
            up[V + V * V + v, at] = wide[v, planes - 1, middle]
        for x in range(planes - 2, -1, -1):
            carried = matvec(lambda i, j: inverse[0, i, j, x, at], matvec(ja, previous))
            previous = [forward[v, x] - carried[v] for v in range(V)]
        for v in range(V):
            down[v, at] = previous[v]
        return carry

    lax.fori_loop(0, columns // 8, one_strip, 0)


def first_kernel(ghost, up, down, right, left, entry, onward, packed):
    slab = lax.axis_index("slab")

    @pl.when(slab == 0)
    def _():
        moved = matvec(stacked(up, V), planes_of(ghost, 0))
        leaving = [up[v] + moved[v] for v in range(V)]
        put(entry, 0, leaving)
        put(onward, 0, leaving)
        put(onward, V, planes_of(up, V + V * V))

    @pl.when(slab == 3)
    def _():
        packed[V:] = left[...]
        moved = matvec(stacked(right, 0), planes_of(ghost, 0))
        for v in range(V):
            packed[v] = jnp.where(lax.axis_index("row") == 0, down[v] + moved[v], down[v])


def lower_kernel(to_one, begun, right, lower):
    @pl.when(lax.axis_index("slab") == 1)
    def _():
        moved = matvec(stacked(right, 0), planes_of(to_one, 0))
        put(lower, 0, [begun[v] + moved[v] for v in range(V)])


def middle_kernel(came, came_side, up_other, side_other, up, down, right, left, lower, third, second, top):
    slab = lax.axis_index("slab")

    @pl.when(slab == 1)
    def _():
        moved = matvec(stacked(left, 0), planes_of(came_side, 0))
        put(lower, 0, [down[v] + moved[v] for v in range(V)])

    @pl.when(slab == 2)
    def _():
        moved = matvec(stacked(up_other, V), planes_of(came, 0))
        inflow = [up_other[v] + moved[v] for v in range(V)]
        moved = matvec(stacked(up, V), inflow)
        onward = [up[v] + moved[v] for v in range(V)]
        moved = matvec(stacked(side_other, V), onward)
        beyond = [side_other[v] + moved[v] for v in range(V)]
        moved = matvec(stacked(left, 0), inflow)
        again = matvec(stacked(right, 0), beyond)
        put(lower, 0, [down[v] + moved[v] + again[v] for v in range(V)])
        put(third, 0, onward)
        put(third, V, planes_of(up, V + V * V))
        put(second, 0, inflow)
        put(top, 0, beyond)


def last_kernel(
    planes, axial, ghost, up_other, came_side, to_third, to_zero, to_one, second, top,
    partial, inverse, state, residual, new_state, forward, inflow, beyond, under,
):
    row = lax.axis_index("row")
    slab = lax.axis_index("slab")
    ja = halved(axial)
    has_top = jnp.where((row == 0) & (slab == 3), 1.0, 0.0)

    at = pl.ds(pl.multiple_of(pl.program_id(0) * 8, 8), 8)

    def fetch(ref, base=0):
        return [ref[base + v, at] for v in range(V)]

    @pl.when(slab == 0)
    def _():
        put(inflow, 0, fetch(ghost))
        put(under, 0, fetch(ghost))
        put(beyond, 0, fetch(to_zero))

    @pl.when(slab == 1)
    def _():
        put(inflow, 0, fetch(came_side))
        put(under, 0, fetch(came_side, V))
        put(beyond, 0, fetch(to_one))

    @pl.when(slab == 2)
    def _():
        put(inflow, 0, fetch(second))
        put(under, 0, fetch(up_other, V + V * V))
        put(beyond, 0, fetch(top))

    @pl.when(slab == 3)
    def _():
        put(inflow, 0, fetch(to_third))
        put(under, 0, fetch(to_third, V))
        put(beyond, 0, [jnp.zeros((8, 128), F32)] * V)

    previous = planes_of(inflow, 0)
    for x in range(planes):
        values = [partial[v, x, at] for v in range(V)]
        if x == planes - 1:
            top_part = matvec(ja, [ghost[v, at] * has_top for v in range(V)])
            values = [values[v] - top_part[v] for v in range(V)]
        if x == 0:
            bottom = matvec(ja, planes_of(under, 0))
            for v in range(V):
                residual[0, v, x] = values[v] + bottom[v]
        else:
            for v in range(V):
                residual[0, v, x] = values[v]
        carried = matvec(ja, previous)
        values = [values[v] + carried[v] for v in range(V)]
        previous = matvec(lambda i, j: inverse[0, i, j, x, at], values)
        for v in range(V):
            forward[v, x] = previous[v]
    following = planes_of(beyond, 0)
    for x in range(planes - 1, -1, -1):
        carried = matvec(lambda i, j: inverse[0, i, j, x, at], matvec(ja, following))
        following = [forward[v, x] - carried[v] for v in range(V)]
        for v in range(V):
            new_state[0, v, x] = state[0, v, x, at] + following[v]


def near(*shape):
    return pltpu.VMEM(shape, F32)


def sds(*shape):
    return jax.ShapeDtypeStruct(shape, F32)


SCALARS = pl.BlockSpec(memory_space=pltpu.SMEM)
WHOLE = pl.BlockSpec(memory_space=pltpu.VMEM)


def params(**more):
    return pltpu.CompilerParams(vmem_limit_bytes=VMEM_BYTES, **more)


def cost(amount):
    return pl.CostEstimate(flops=amount, bytes_accessed=amount // 8, transcendentals=0)


def per_device(state, source, diag_inverse, jac_axial, jac_cross, owner):
    planes, columns, radial = state.shape[2:]
    sectors = lax.axis_size("sector")
    slabs = lax.axis_size("slab")
    plane = (V, columns, radial)
    cells = pl.BlockSpec((1, V, planes, 8, radial), lambda i: (0, 0, 0, i, 0))
    size = slabs * sectors

    def device(row, sector, slab):
        return row * size + sector % sectors * slabs + slab

    def import_pairs(even):
        pairs = []
        for j in range(sectors):
            pairs.append((device(1, j, 0), device(0, j - even, slabs - 1)))
            pairs.append((device(0, j, slabs - 1), device(1, j + even + 2, 0)))
        return pairs

    two_down = []
    for j in range(sectors):
        two_down.append((device(0, j, slabs - 1), device(0, j - 2, slabs - 1)))
        two_down.append((device(1, j, 0), device(1, j - 2, 0)))

    total = sectors * columns
    assert total & (total - 1) == 0 and columns & (columns - 1) == 0
    axial = jnp.transpose(jac_axial, (1, 0, 2))
    cross = jnp.transpose(jac_cross[0], (1, 0, 2))
    towards_low, interface, towards_high, lowest = pl.pallas_call(
        lambda *refs: pack_kernel(planes, columns, *refs),
        out_shape=(near(V, planes + columns, radial), near(*plane), near(V, planes, radial), near(*plane)),
        compiler_params=params(),
        name="pack",
    )(state)
    above = lax.ppermute(lowest, "slab", [(k, k - 1) for k in range(1, slabs)])
    from_low = lax.ppermute(towards_high, "sector", [(j, (j + 1) % sectors) for j in range(sectors)])
    from_second = lax.ppermute(interface, AXES, two_down)
    from_high = lax.ppermute(towards_low, "sector", [(j, (j - 1) % sectors) for j in range(sectors)])

    square = near(V * V, columns, radial)
    blocks = pl.pallas_call(
        load_kernel,
        in_specs=[pl.BlockSpec(memory_space=pltpu.HBM), pl.BlockSpec(memory_space=pl.ANY)],
        out_specs=WHOLE,
        out_shape=near(*diag_inverse.shape),
        scratch_shapes=[pltpu.SemaphoreType.DMA],
        compiler_params=params(),
        cost_estimate=cost(20_000_000),
        name="load",
    )(pltpu.with_memory_space_constraint(diag_inverse, pltpu.HBM), lowest)
    message, pair = pl.pallas_call(
        lambda *refs: window_kernel(planes, columns, sectors, *refs),
        in_specs=[SCALARS] + [WHOLE] * 3,
        out_specs=[WHOLE, SCALARS],
        out_shape=(near(*plane), jax.ShapeDtypeStruct((1,), jnp.int32)),
        scratch_shapes=[
            pltpu.VMEM((V, 3 * columns, radial), F32),
            pltpu.VMEM((V, columns + 8, radial), F32),
        ],
        compiler_params=params(),
        name="window",
    )(owner, interface, from_high, from_second)

    def exchange(even, message, from_low, above, from_high, blocks):
        ghost = lax.ppermute(message, AXES, import_pairs(even))
        prefix, right, left = pl.pallas_call(
            lambda *refs: matrix_kernel(planes, *refs),
            in_specs=[WHOLE, WHOLE],
            out_shape=(square, square, square),
            scratch_shapes=[
                pltpu.VMEM((planes, V * V, 8, radial), F32),
                pltpu.VMEM((planes, V * V, 8, radial), F32),
                pltpu.VMEM((V * V, 8, radial), F32),
                pltpu.VMEM((V * V, 8, radial), F32),
            ],
            compiler_params=params(),
            cost_estimate=cost(60_000_000),
            name="matrices",
        )(axial, blocks)
        partial, up, down = pl.pallas_call(
            lambda *refs: residual_kernel(planes, columns, *refs),
            in_specs=[WHOLE] * 9,
            out_shape=(
                near(V, planes, columns, radial), near(2 * V + V * V, columns, radial), near(*plane),
            ),
            scratch_shapes=[
                pltpu.VMEM((V, planes, columns + 16, radial), F32),
                pltpu.VMEM((V, planes, 8, radial), F32),
            ],
            compiler_params=params(),
            cost_estimate=cost(40_000_000),
            name="residual",
        )(axial, cross, state, source, blocks, from_high, from_low, above, prefix)
        return ghost, partial, up, down, right, left

    ghost, partial, up, down, right, left = lax.switch(
        pair[0],
        [lambda *args, e=e: exchange(2 * e, *args) for e in range(sectors // 2)],
        message, from_low, above, from_high, blocks,
    )
    up_other = lax.ppermute(up, "slab", [(1, 2)])
    entry, side_message, packed = pl.pallas_call(
        first_kernel,
        out_shape=(near(*plane), near(2 * V, columns, radial), near(V + V * V, columns, radial)),
        compiler_params=params(),
        name="first",
    )(ghost, up, down, right, left)
    side_other = lax.ppermute(packed, "slab", [(3, 2)])
    came = lax.ppermute(entry, "slab", [(0, 2)])
    side_message, came = lax.optimization_barrier((side_message, came))
    came_side = lax.ppermute(side_message, "slab", [(0, 1)])
    lower, onward, second, top = pl.pallas_call(
        middle_kernel,
        out_shape=(near(*plane), near(2 * V, columns, radial), near(*plane), near(*plane)),
        compiler_params=params(),
        name="middle",
    )(came, came_side, up_other, side_other, up, down, right, left)
    to_one = lax.ppermute(lower, "slab", [(2, 1)])
    onward, arrived = lax.optimization_barrier((onward, to_one))
    to_third = lax.ppermute(onward, "slab", [(2, 3)])
    lowest_update = pl.pallas_call(
        lower_kernel,
        out_shape=near(*plane),
        compiler_params=params(),
        name="lower",
    )(to_one, lower, right)
    to_zero = lax.ppermute(lowest_update, "slab", [(1, 0)])

    residual, new_state = pl.pallas_call(
        lambda *refs: last_kernel(planes, *refs),
        grid=(columns // 8,),
        in_specs=[WHOLE] * 12,
        out_specs=(cells, cells),
        out_shape=(sds(*state.shape), sds(*state.shape)),
        scratch_shapes=[pltpu.VMEM((V, planes, 8, radial), F32)] + [pltpu.VMEM((V, 8, radial), F32)] * 3,
        compiler_params=params(),
        name="last",
    )(
        axial, ghost, up_other, came_side, to_third, to_zero, arrived, second, top,
        partial, blocks, state,
    )
    return residual, new_state


def solution(mesh):
    return jax.shard_map(
        per_device,
        mesh=mesh,
        in_specs=(
            P("row", None, "slab", "sector", None),
            P("row", None, "slab", "sector", None),
            P("row", None, None, "slab", "sector", None),
            P("row", None, None),
            P("row", None, None, None),
            P(),
        ),
        out_specs=(P("row", None, "slab", "sector", None), P("row", None, "slab", "sector", None)),
        check_vma=False,
    )
```

```python
import jax
import jax.numpy as jnp
from jax import lax
from jax.experimental import pallas as pl
from jax.experimental.pallas import tpu as pltpu
from jax.sharding import PartitionSpec as P

F32 = jnp.float32
V = 5
AXES = ("row", "sector", "slab")
VMEM_BYTES = 14 * 1024 * 1024


def matvec(mat, vec):
    out = []
    for i in range(V):
        acc = mat(i, 0) * vec[0]
        for j in range(1, V):
            acc = acc + mat(i, j) * vec[j]
        out.append(acc)
    return out


def stacked(ref, base):
    return lambda i, j: ref[base + V * i + j]


def planes_of(ref, base):
    return [ref[base + v] for v in range(V)]


def put(ref, base, values):
    for v in range(V):
        ref[base + v] = values[v]


def sliding(owner, columns, total):
    lead = owner[0]

    def lower(i, best):
        return jnp.minimum(best, ((owner[i] - lead + total // 2) & (total - 1)) - total // 2)

    return (lead + lax.fori_loop(1, columns, lower, jnp.int32(0), unroll=True)) & (total - 1)


def pack_kernel(
    planes, columns, state, towards_low, interface, towards_high, lowest,
):
    row = lax.axis_index("row")
    face = jnp.where(row == 0, planes - 1, 0)
    for v in range(V):
        plane = state[0, v, face]
        interface[v] = plane
        towards_low[v, planes:] = plane
        lowest[v] = state[0, v, 0]
        for x in range(planes):
            towards_low[v, x : x + 1] = state[0, v, x, 0:1]
            towards_high[v, x : x + 1] = state[0, v, x, columns - 1 : columns]


def load_kernel(inverse, lowest, blocks, arrived):
    copy = pltpu.make_async_copy(inverse, blocks, arrived)
    copy.start()
    copy.wait()


def halved(ref, which=0):
    entries = [
        [jnp.broadcast_to(0.5 * ref[i, which : which + 1, j : j + 1], (8, 128)) for j in range(V)]
        for i in range(V)
    ]
    return lambda i, j: entries[i][j]


def window_kernel(planes, columns, sectors, owner, own, next_one, next_two, message, pair, table, landing):
    row = lax.axis_index("row")
    sector = lax.axis_index("sector")
    total = sectors * columns
    for v in range(V):
        table[v, 0:columns] = own[v]
        table[v, columns : 2 * columns] = next_one[v, planes:]
        table[v, 2 * columns :] = next_two[v]
    turn = sliding(owner, columns, total) >> (columns.bit_length() - 1)
    even = turn & -2
    pair[0] = turn >> 1

    @pl.when(row == 1)
    def _():
        facing = (sector - even) & (sectors - 1)

        def step(i, carry):
            at = (owner[facing * columns + i] - sector * columns) & (total - 1)
            at = jnp.minimum(at, 3 * columns - 1)
            for v in range(V):
                landing[v, pl.ds(i, 1)] = table[v, pl.ds(at, 1)]
            return carry

        lax.fori_loop(0, columns, step, 0, unroll=8)

    @pl.when(row == 0)
    def _():
        facing = (sector + even + 2) & (sectors - 1)
        first = (1 - (turn - even)) * columns

        def step(i, carry):
            at = first + i
            column = owner[(sector * columns + at) & (total - 1)]
            to = jnp.minimum((column - facing * columns) & (total - 1), columns)
            for v in range(V):
                landing[v, pl.ds(to, 1)] = table[v, pl.ds(at, 1)]
            return carry

        lax.fori_loop(0, 2 * columns, step, 0, unroll=8)

    for v in range(V):
        message[v] = landing[v, 0:columns]


def matrix_kernel(
    planes, axial, inverse, prefix_out, right, left, product, prefix, left_now, right_now,
):
    row = lax.axis_index("row")
    slab = lax.axis_index("slab")
    scaled = halved(axial)

    def one_strip(step, carry):
        at = pl.ds(pl.multiple_of(step * 8, 8), 8)

        def factor(x):
            return lambda i, j: product[x, V * i + j]

        def flux_times(x):
            for i in range(V):
                entries = [inverse[0, i, k, x, at] for k in range(V)]
                for j in range(V):
                    acc = entries[0] * scaled(0, j)
                    for k in range(1, V):
                        acc = acc + entries[k] * scaled(k, j)
                    product[x, V * i + j] = acc

        def forward(x, carry):
            flux_times(x)
            for j in range(V):
                column = [prefix[x - 1, V * i + j] for i in range(V)]
                put_column(prefix.at[x], j, matvec(factor(x), column))
            return carry

        flux_times(0)
        for k in range(V * V):
            prefix[0, k] = product[0, k]
        lax.fori_loop(1, planes, forward, 0)
        for k in range(V * V):
            prefix_out[k, at] = prefix[planes - 1, k]

        @pl.when(slab > 0)
        def _():
            for j in range(V):
                column = [prefix[planes - 2, V * i + j] for i in range(V)]
                put_column(left_now, j, matvec(factor(planes - 1), column))

            def backward(step, carry):
                x = planes - 1 - step
                for j in range(V):
                    column = [prefix[x - 1, V * i + j] - left_now[V * i + j] for i in range(V)]
                    put_column(left_now, j, matvec(factor(x), column))
                return carry

            lax.fori_loop(1, planes - 1, backward, 0)
            for j in range(V):
                column = [float(i == j) - left_now[V * i + j] for i in range(V)]
                put_column(left_now, j, matvec(factor(0), column))
            for k in range(V * V):
                left[k, at] = left_now[k]

        @pl.when((slab == 1) | (slab == 2) | ((slab == 3) & (row == 0)))
        def _():
            for k in range(V * V):
                right_now[k] = product[planes - 1, k]

            def backward(step, carry):
                x = planes - 1 - step
                for j in range(V):
                    column = [right_now[V * i + j] for i in range(V)]
                    put_column(right_now, j, matvec(factor(x), column))
                return carry

            lax.fori_loop(1, planes, backward, 0)
            for k in range(V * V):
                right[k, at] = right_now[k]

        return carry

    lax.fori_loop(0, inverse.shape[4] // 8, one_strip, 0)


def put_column(ref, j, values):
    for i in range(V):
        ref[V * i + j] = values[i]


def residual_kernel(
    planes, columns, axial, cross, state, source, inverse, from_high, from_low, above, prefix_in,
    residual, up, down, wide, forward,
):
    for v in range(V):
        for x in range(planes):
            wide[v, x, 8 : 8 + columns] = state[0, v, x]
            wide[v, x, 7:8] = from_low[v, x : x + 1]
            wide[v, x, 8 + columns : 9 + columns] = from_high[v, x : x + 1]
    rows = lax.broadcasted_iota(jnp.int32, (8, 128), 0)
    lanes = lax.broadcasted_iota(jnp.int32, (8, 128), 1)
    ja = halved(axial)
    jb = halved(cross)
    jr = halved(cross, 1)

    def one_strip(step, carry):
        at = pl.ds(pl.multiple_of(step * 8, 8), 8)
        middle = pl.ds(pl.multiple_of(step * 8 + 8, 8), 8)
        high = pl.ds(pl.multiple_of(step * 8 + 16, 8), 8)
        previous = None
        for x in range(planes):
            along, around, outward = [], [], []
            for v in range(V):
                here = wide[v, x, middle]
                nearer = wide[v, x + 1, middle] if x + 1 < planes else above[v, at]
                along.append(nearer - wide[v, x - 1, middle] if x else nearer)
                plus = jnp.where(rows == 0, wide[v, x, high], here)
                minus = jnp.where(rows == 7, wide[v, x, at], here)
                around.append(pltpu.roll(plus, 7, 0) - pltpu.roll(minus, 1, 0))
                outward.append(
                    jnp.where(lanes == 127, 0.0, pltpu.roll(here, 127, 1))
                    - jnp.where(lanes == 0, 0.0, pltpu.roll(here, 1, 1))
                )
            one, two, three = matvec(ja, along), matvec(jb, around), matvec(jr, outward)
            values = [source[0, v, x, at] - (one[v] + two[v] + three[v]) for v in range(V)]
            for v in range(V):
                residual[v, x, at] = values[v]
            if previous is not None:
                carried = matvec(ja, previous)
                values = [values[v] + carried[v] for v in range(V)]
            previous = matvec(lambda i, j: inverse[0, i, j, x, at], values)
            for v in range(V):
                forward[v, x] = previous[v]
        for v in range(V):
            last = wide[v, planes - 1, middle]
            up[v, at] = previous[v] + last
        for k in range(V * V):
            up[V + k, at] = prefix_in[k, at]
        for v in range(V):
            up[V + V * V + v, at] = wide[v, planes - 1, middle]
        for x in range(planes - 2, -1, -1):
            carried = matvec(lambda i, j: inverse[0, i, j, x, at], matvec(ja, previous))
            previous = [forward[v, x] - carried[v] for v in range(V)]
        for v in range(V):
            down[v, at] = previous[v]
        return carry

    lax.fori_loop(0, columns // 8, one_strip, 0)


def first_kernel(ghost, up, down, right, left, entry, onward, packed):
    slab = lax.axis_index("slab")

    @pl.when(slab == 0)
    def _():
        moved = matvec(stacked(up, V), planes_of(ghost, 0))
        leaving = [up[v] + moved[v] for v in range(V)]
        put(entry, 0, leaving)
        put(onward, 0, leaving)
        put(onward, V, planes_of(up, V + V * V))

    @pl.when(slab == 3)
    def _():
        packed[V:] = left[...]
        moved = matvec(stacked(right, 0), planes_of(ghost, 0))
        for v in range(V):
            packed[v] = jnp.where(lax.axis_index("row") == 0, down[v] + moved[v], down[v])


def lower_kernel(to_one, came_side, down, right, left, lower):
    @pl.when(lax.axis_index("slab") == 1)
    def _():
        moved = matvec(stacked(left, 0), planes_of(came_side, 0))
        again = matvec(stacked(right, 0), planes_of(to_one, 0))
        put(lower, 0, [down[v] + moved[v] + again[v] for v in range(V)])


def middle_kernel(came, up_other, side_other, up, down, right, left, lower, third, second, top):
    slab = lax.axis_index("slab")

    @pl.when(slab == 2)
    def _():
        moved = matvec(stacked(up_other, V), planes_of(came, 0))
        inflow = [up_other[v] + moved[v] for v in range(V)]
        moved = matvec(stacked(up, V), inflow)
        onward = [up[v] + moved[v] for v in range(V)]
        moved = matvec(stacked(side_other, V), onward)
        beyond = [side_other[v] + moved[v] for v in range(V)]
        moved = matvec(stacked(left, 0), inflow)
        again = matvec(stacked(right, 0), beyond)
        put(lower, 0, [down[v] + moved[v] + again[v] for v in range(V)])
        put(third, 0, onward)
        put(third, V, planes_of(up, V + V * V))
        put(second, 0, inflow)
        put(top, 0, beyond)


def last_kernel(
    planes, axial, ghost, up_other, came_side, to_third, to_zero, to_one, second, top,
    partial, inverse, state, residual, new_state, forward, inflow, beyond, under,
):
    row = lax.axis_index("row")
    slab = lax.axis_index("slab")
    ja = halved(axial)
    has_top = jnp.where((row == 0) & (slab == 3), 1.0, 0.0)

    at = pl.ds(pl.multiple_of(pl.program_id(0) * 8, 8), 8)

    def fetch(ref, base=0):
        return [ref[base + v, at] for v in range(V)]

    @pl.when(slab == 0)
    def _():
        put(inflow, 0, fetch(ghost))
        put(under, 0, fetch(ghost))
        put(beyond, 0, fetch(to_zero))

    @pl.when(slab == 1)
    def _():
        put(inflow, 0, fetch(came_side))
        put(under, 0, fetch(came_side, V))
        put(beyond, 0, fetch(to_one))

    @pl.when(slab == 2)
    def _():
        put(inflow, 0, fetch(second))
        put(under, 0, fetch(up_other, V + V * V))
        put(beyond, 0, fetch(top))

    @pl.when(slab == 3)
    def _():
        put(inflow, 0, fetch(to_third))
        put(under, 0, fetch(to_third, V))
        put(beyond, 0, [jnp.zeros((8, 128), F32)] * V)

    previous = planes_of(inflow, 0)
    for x in range(planes):
        values = [partial[v, x, at] for v in range(V)]
        if x == planes - 1:
            top_part = matvec(ja, [ghost[v, at] * has_top for v in range(V)])
            values = [values[v] - top_part[v] for v in range(V)]
        if x == 0:
            bottom = matvec(ja, planes_of(under, 0))
            for v in range(V):
                residual[0, v, x] = values[v] + bottom[v]
        else:
            for v in range(V):
                residual[0, v, x] = values[v]
        carried = matvec(ja, previous)
        values = [values[v] + carried[v] for v in range(V)]
        previous = matvec(lambda i, j: inverse[0, i, j, x, at], values)
        for v in range(V):
            forward[v, x] = previous[v]
    following = planes_of(beyond, 0)
    for x in range(planes - 1, -1, -1):
        carried = matvec(lambda i, j: inverse[0, i, j, x, at], matvec(ja, following))
        following = [forward[v, x] - carried[v] for v in range(V)]
        for v in range(V):
            new_state[0, v, x] = state[0, v, x, at] + following[v]


def near(*shape):
    return pltpu.VMEM(shape, F32)


def sds(*shape):
    return jax.ShapeDtypeStruct(shape, F32)


SCALARS = pl.BlockSpec(memory_space=pltpu.SMEM)
WHOLE = pl.BlockSpec(memory_space=pltpu.VMEM)


def params(**more):
    return pltpu.CompilerParams(vmem_limit_bytes=VMEM_BYTES, **more)


def cost(amount):
    return pl.CostEstimate(flops=amount, bytes_accessed=amount // 8, transcendentals=0)


def per_device(state, source, diag_inverse, jac_axial, jac_cross, owner):
    planes, columns, radial = state.shape[2:]
    sectors = lax.axis_size("sector")
    slabs = lax.axis_size("slab")
    plane = (V, columns, radial)
    cells = pl.BlockSpec((1, V, planes, 8, radial), lambda i: (0, 0, 0, i, 0))
    size = slabs * sectors

    def device(row, sector, slab):
        return row * size + sector % sectors * slabs + slab

    def import_pairs(even):
        pairs = []
        for j in range(sectors):
            pairs.append((device(1, j, 0), device(0, j - even, slabs - 1)))
            pairs.append((device(0, j, slabs - 1), device(1, j + even + 2, 0)))
        return pairs

    two_down = []
    for j in range(sectors):
        two_down.append((device(0, j, slabs - 1), device(0, j - 2, slabs - 1)))
        two_down.append((device(1, j, 0), device(1, j - 2, 0)))

    total = sectors * columns
    assert total & (total - 1) == 0 and columns & (columns - 1) == 0
    axial = jnp.transpose(jac_axial, (1, 0, 2))
    cross = jnp.transpose(jac_cross[0], (1, 0, 2))
    towards_low, interface, towards_high, lowest = pl.pallas_call(
        lambda *refs: pack_kernel(planes, columns, *refs),
        out_shape=(near(V, planes + columns, radial), near(*plane), near(V, planes, radial), near(*plane)),
        compiler_params=params(),
        name="pack",
    )(state)
    above = lax.ppermute(lowest, "slab", [(k, k - 1) for k in range(1, slabs)])
    from_low = lax.ppermute(towards_high, "sector", [(j, (j + 1) % sectors) for j in range(sectors)])
    from_second = lax.ppermute(interface, AXES, two_down)
    from_high = lax.ppermute(towards_low, "sector", [(j, (j - 1) % sectors) for j in range(sectors)])

    square = near(V * V, columns, radial)
    blocks = pl.pallas_call(
        load_kernel,
        in_specs=[pl.BlockSpec(memory_space=pltpu.HBM), pl.BlockSpec(memory_space=pl.ANY)],
        out_specs=WHOLE,
        out_shape=near(*diag_inverse.shape),
        scratch_shapes=[pltpu.SemaphoreType.DMA],
        compiler_params=params(),
        cost_estimate=cost(20_000_000),
        name="load",
    )(pltpu.with_memory_space_constraint(diag_inverse, pltpu.HBM), lowest)
    message, pair = pl.pallas_call(
        lambda *refs: window_kernel(planes, columns, sectors, *refs),
        in_specs=[SCALARS] + [WHOLE] * 3,
        out_specs=[WHOLE, SCALARS],
        out_shape=(near(*plane), jax.ShapeDtypeStruct((1,), jnp.int32)),
        scratch_shapes=[
            pltpu.VMEM((V, 3 * columns, radial), F32),
            pltpu.VMEM((V, columns + 8, radial), F32),
        ],
        compiler_params=params(),
        name="window",
    )(owner, interface, from_high, from_second)

    def exchange(even, message, from_low, above, from_high, blocks):
        ghost = lax.ppermute(message, AXES, import_pairs(even))
        prefix, right, left = pl.pallas_call(
            lambda *refs: matrix_kernel(planes, *refs),
            in_specs=[WHOLE, WHOLE],
            out_shape=(square, square, square),
            scratch_shapes=[
                pltpu.VMEM((planes, V * V, 8, radial), F32),
                pltpu.VMEM((planes, V * V, 8, radial), F32),
                pltpu.VMEM((V * V, 8, radial), F32),
                pltpu.VMEM((V * V, 8, radial), F32),
            ],
            compiler_params=params(),
            cost_estimate=cost(60_000_000),
            name="matrices",
        )(axial, blocks)
        partial, up, down = pl.pallas_call(
            lambda *refs: residual_kernel(planes, columns, *refs),
            in_specs=[WHOLE] * 9,
            out_shape=(
                near(V, planes, columns, radial), near(2 * V + V * V, columns, radial), near(*plane),
            ),
            scratch_shapes=[
                pltpu.VMEM((V, planes, columns + 16, radial), F32),
                pltpu.VMEM((V, planes, 8, radial), F32),
            ],
            compiler_params=params(),
            cost_estimate=cost(40_000_000),
            name="residual",
        )(axial, cross, state, source, blocks, from_high, from_low, above, prefix)
        return ghost, partial, up, down, right, left

    ghost, partial, up, down, right, left = lax.switch(
        pair[0],
        [lambda *args, e=e: exchange(2 * e, *args) for e in range(sectors // 2)],
        message, from_low, above, from_high, blocks,
    )
    up_other = lax.ppermute(up, "slab", [(1, 2)])
    entry, side_message, packed = pl.pallas_call(
        first_kernel,
        out_shape=(near(*plane), near(2 * V, columns, radial), near(V + V * V, columns, radial)),
        compiler_params=params(),
        name="first",
    )(ghost, up, down, right, left)
    side_other = lax.ppermute(packed, "slab", [(3, 2)])
    came = lax.ppermute(entry, "slab", [(0, 2)])
    side_message, came = lax.optimization_barrier((side_message, came))
    came_side = lax.ppermute(side_message, "slab", [(0, 1)])
    lower, onward, second, top = pl.pallas_call(
        middle_kernel,
        out_shape=(near(*plane), near(2 * V, columns, radial), near(*plane), near(*plane)),
        compiler_params=params(),
        name="middle",
    )(came, up_other, side_other, up, down, right, left)
    to_one = lax.ppermute(lower, "slab", [(2, 1)])
    onward, arrived = lax.optimization_barrier((onward, to_one))
    to_third = lax.ppermute(onward, "slab", [(2, 3)])
    lowest_update = pl.pallas_call(
        lower_kernel,
        out_shape=near(*plane),
        compiler_params=params(),
        name="lower",
    )(to_one, came_side, down, right, left)
    to_zero = lax.ppermute(lowest_update, "slab", [(1, 0)])

    residual, new_state = pl.pallas_call(
        lambda *refs: last_kernel(planes, *refs),
        grid=(columns // 8,),
        in_specs=[WHOLE] * 12,
        out_specs=(cells, cells),
        out_shape=(sds(*state.shape), sds(*state.shape)),
        scratch_shapes=[pltpu.VMEM((V, planes, 8, radial), F32)] + [pltpu.VMEM((V, 8, radial), F32)] * 3,
        compiler_params=params(),
        name="last",
    )(
        axial, ghost, up_other, came_side, to_third, to_zero, arrived, second, top,
        partial, blocks, state,
    )
    return residual, new_state


def solution(mesh):
    return jax.shard_map(
        per_device,
        mesh=mesh,
        in_specs=(
            P("row", None, "slab", "sector", None),
            P("row", None, "slab", "sector", None),
            P("row", None, None, "slab", "sector", None),
            P("row", None, None),
            P("row", None, None, None),
            P(),
        ),
        out_specs=(P("row", None, "slab", "sector", None), P("row", None, "slab", "sector", None)),
        check_vma=False,
    )
```
